512 devices in a mesh: comp: 8 (over y), blk: 64 (over z, x, core).
Axes of the slice: x: 4, y: 8, z: 8, core: 2. Of those that a mesh axis runs over, the one named last changes fastest.
Arguments:
- base_state: float32 [8, 64, 6, 2, 128, 128], P('comp', 'blk'), may hold values from -1.2 to 5.2, as said below
- section_state: float32 [8, 64, 6, 2, 128, 128], P('comp', 'blk'), may hold values from -1.2 to 5.2, as said below
- volume: float32 [8, 64, 2, 128, 128], P('comp', 'blk'), may hold values from 0.25 to 12, as said below
- distance: float32 [8, 64, 2, 128, 128], P('comp', 'blk'), may hold values from 0.5 to 3
- orientation: int32 [8, 64, 3], replicated, may hold values from 0 to 1
Outputs:
- new_state: float32 [8, 64, 6, 2, 128, 128], P('comp', 'blk')
- residual_norm: float32 [], replicated
The draws below stay inside these ranges and needn't reach their ends.
Inputs may be any that keep to these rules, and one draw needn't show every extreme that they name: `base_state`: a valid flow in every cell of every block: density between 0.6 and 1.4, pressure 0.4 (E - |m|^2 / (2 rho)) between 0.5 and 1.5, and a positive last field. `section_state`: a valid flow in every cell of every block, with the same bounds as base_state. `volume`: positive volumes.
All inputs are finite; a program needn't handle non-finite values.
Results may differ from the reference program's by a relative error of at most 0.0003.
Values sent between devices are 32-bit elements; how exact they have to be, the bound alone decides.
A program may use at most 64 MiB of HBM per device.

```python
import math
import jax
import jax.numpy as jnp
from jax import lax

DEPTH = 2
FACE = 128
GROUPS = 8
CHAIN = 64


ADIABATIC_INDEX = 1.4


def flow_state(key):
    shape = (GROUPS, CHAIN, DEPTH, FACE, FACE)
    keys = jax.random.split(key, 4)
    fluid_compactness = jax.random.uniform(keys[0], shape, jnp.float32, 0.7, 1.3)
    velocity = 0.3 * jax.random.truncated_normal(keys[1], -3.0, 3.0, (3,) + shape, jnp.float32)
    thermodynamic_stress = jax.random.uniform(keys[2], shape, jnp.float32, 0.6, 1.4)
    eddy_share = jnp.exp(jax.random.uniform(keys[3], shape, jnp.float32, jnp.log(0.02), jnp.log(0.5)))
    squared = velocity[0] * velocity[0] + velocity[1] * velocity[1] + velocity[2] * velocity[2]
    energy = thermodynamic_stress / (ADIABATIC_INDEX - 1.0) + 0.5 * fluid_compactness * squared
    fields = [fluid_compactness, fluid_compactness * velocity[0], fluid_compactness * velocity[1], fluid_compactness * velocity[2], energy, fluid_compactness * eddy_share]
    return jnp.stack(fields, axis=2).astype(jnp.float32)


def draw_base_state(key, part):
    return flow_state(jax.random.fold_in(key, 11))


def draw_section_state(key, part):
    return flow_state(jax.random.fold_in(key, 23))


def draw_volume(key, part):
    shape = (GROUPS, CHAIN, DEPTH, FACE, FACE)
    total = GROUPS * CHAIN
    order = jnp.arange(total, dtype=jnp.float32).reshape((GROUPS, CHAIN))
    trend = 3.0 - 2.0 * order / max(total - 1, 1)
    block_key = jax.random.fold_in(key, 41)
    block_factor = jnp.exp(jax.random.uniform(block_key, (GROUPS, CHAIN), jnp.float32, jnp.log(0.5), jnp.log(2.0)))
    inner_key = jax.random.fold_in(key, 37)
    rough = jnp.exp(jax.random.uniform(inner_key, shape, jnp.float32, jnp.log(0.5), jnp.log(2.0)))
    scale = trend * block_factor
    return (scale[:, :, None, None, None] * rough).astype(jnp.float32)


def with_ends(values, own_key, least, top_value):
    dims = values.shape
    spot = [jax.random.randint(jax.random.fold_in(own_key, axis), (), 0, dims[axis]) for axis in range(len(dims))]
    values = values.at[tuple(spot)].set(least)
    longest = dims.index(max(dims))
    spot[longest] = (spot[longest] + 1) % dims[longest]
    return values.at[tuple(spot)].set(top_value)


def levels(key, extent, cuts, low, high):
    loudness = 1.0
    for axis_at, parts in cuts:
        draws = jax.random.uniform(jax.random.fold_in(jax.random.fold_in(key, 6), axis_at), (parts,), jnp.float32, low / len(cuts), high / len(cuts))
        loudness = loudness * jnp.repeat(jnp.exp(draws), extent[axis_at] // parts).reshape((-1,) + (1,) * (len(extent) - 1 - axis_at))
    return loudness


def setup_inputs(seed: int = 0) -> dict:
    arg_keys = jax.random.split(jax.random.key(seed), 6)
    base_state = draw_base_state(jax.random.fold_in(arg_keys[5], 71), 0)
    section_state = draw_section_state(jax.random.fold_in(arg_keys[5], 71), 0)
    volume = draw_volume(jax.random.fold_in(arg_keys[5], 71), 0)
    distance = jnp.clip(jnp.exp(math.log(3.0) - 1.7917595 * jax.random.uniform(arg_keys[3], (GROUPS, CHAIN, DEPTH, FACE, FACE), jnp.float32) ** levels(arg_keys[3], (GROUPS, CHAIN, DEPTH, FACE, FACE), ((0, 8), (1, 64)), -0.2, 0.2)), 0.5, 3.0)
    orientation = with_ends(jax.random.randint(arg_keys[4], (GROUPS, CHAIN, 3), 0, 2), jax.random.fold_in(arg_keys[4], 1), 0, 1).astype(jnp.int32)
    return dict(base_state=base_state, section_state=section_state, volume=volume, distance=distance, orientation=orientation)


ADIABATIC_INDEX = 1.4
SENSOR_GAIN = 0.25
FOURTH_GAIN = 0.03125
VISCOSITY = 0.05
DIFFUSIVITY_QUOT = 0.72
DIFFUSE_SIGMA = 0.6666666666666666
PRODUCE_GAIN = 0.1355
DESTROY_GAIN = 3.239
DAMPING_CONST = 7.1
COURANT = 2.0
SECTION_WEIGHT = 0.5

def take_slab(array, axis, start, count):
    return lax.slice_in_dim(array, start, start + count, axis=axis)

def field_sign(count, field, dtype):
    return jnp.where(jnp.arange(count) == field, -1.0, 1.0).astype(dtype)[:, None, None, None]

def swap_fields(array, second, third):
    order = list(range(array.shape[0]))
    order[second] = third
    order[third] = second
    return jnp.stack([array[field] for field in order])

def reorient(layers, flags, second, third):
    count = layers.shape[0]
    result = jnp.where(flags[1] > 0, jnp.flip(layers, 2) * field_sign(count, second, layers.dtype), layers)
    result = jnp.where(flags[2] > 0, jnp.flip(result, 3) * field_sign(count, third, layers.dtype), result)
    turned = jnp.swapaxes(swap_fields(result, second, third), 2, 3)
    return jnp.where(flags[0] > 0, turned, result)

def restore(layers, flags, second, third):
    count = layers.shape[0]
    turned = jnp.swapaxes(swap_fields(layers, second, third), 2, 3)
    result = jnp.where(flags[0] > 0, turned, layers)
    result = jnp.where(flags[1] > 0, jnp.flip(result, 2) * field_sign(count, second, layers.dtype), result)
    result = jnp.where(flags[2] > 0, jnp.flip(result, 3) * field_sign(count, third, layers.dtype), result)
    return result

def assemble(own, below, above, flags_below, flags_above, first, last, second, third):
    depth = own.shape[1]
    lower = jnp.where(first, jnp.concatenate([own[:, :1], own[:, :1]], axis=1), reorient(below, flags_below, second, third))
    upper = jnp.where(last, jnp.concatenate([own[:, depth - 1:], own[:, depth - 1:]], axis=1), restore(above, flags_above, second, third))
    stacked = jnp.concatenate([lower, own, upper], axis=1)
    return jnp.pad(stacked, ((0, 0), (0, 0), (2, 2), (2, 2)), mode='edge')

def primitive(state):
    fluid_compactness = state[0:1]
    moment = state[1:4]
    velocity = moment / fluid_compactness
    thermodynamic_stress = (ADIABATIC_INDEX - 1.0) * (state[4:5] - 0.5 * (moment[0:1] * velocity[0:1] + moment[1:2] * velocity[1:2] + moment[2:3] * velocity[2:3]))
    eddy_field = state[5:6] / fluid_compactness
    return jnp.concatenate([velocity, thermodynamic_stress, eddy_field], axis=0)

def total_speed(state, prims):
    sound = jnp.sqrt(ADIABATIC_INDEX * prims[3] / state[0])
    return jnp.abs(prims[0]) + sound + (jnp.abs(prims[1]) + sound) + (jnp.abs(prims[2]) + sound)

def crop_others(array, axis):
    for other in (1, 2, 3):
        if other != axis:
            array = take_slab(array, other, 2, array.shape[other] - 4)
    return array

def face_flux(state, prims, axis):
    state = crop_others(state, axis)
    prims = crop_others(prims, axis)
    count = state.shape[axis] - 4
    fluid_compactness = state[0:1]
    thermodynamic_stress = prims[3:4]
    normal = prims[axis - 1:axis]
    speed = jnp.abs(normal) + jnp.sqrt(ADIABATIC_INDEX * thermodynamic_stress / fluid_compactness)
    fields = [state[field] * normal[0] for field in range(6)]
    fields[axis] = fields[axis] + thermodynamic_stress[0]
    fields[4] = fields[4] + thermodynamic_stress[0] * normal[0]
    inviscid = jnp.stack(fields)

    def interface_couple(array):
        return (take_slab(array, axis, 1, count + 1), take_slab(array, axis, 2, count + 1))
    flux_left, flux_right = interface_couple(inviscid)
    central = 0.5 * (flux_left + flux_right)
    before = take_slab(thermodynamic_stress, axis, 0, count + 2)
    middle = take_slab(thermodynamic_stress, axis, 1, count + 2)
    after = take_slab(thermodynamic_stress, axis, 2, count + 2)
    sensor = jnp.abs(after - 2.0 * middle + before) / (after + 2.0 * middle + before)
    second_gain = SENSOR_GAIN * jnp.maximum(take_slab(sensor, axis, 0, count + 1), take_slab(sensor, axis, 1, count + 1))
    fourth_gain = jnp.maximum(0.0, FOURTH_GAIN - second_gain)
    speed_left, speed_right = interface_couple(speed)
    state_left, state_right = interface_couple(state)
    far_left = take_slab(state, axis, 0, count + 1)
    far_right = take_slab(state, axis, 3, count + 1)
    damping = 0.5 * (speed_left + speed_right) * (second_gain * (state_right - state_left) - fourth_gain * (far_right - 3.0 * state_right + 3.0 * state_left - far_left))
    ratio_chi = state[5:6] / VISCOSITY
    cubed = ratio_chi * ratio_chi * ratio_chi
    eddy_viscosity = state[5:6] * cubed / (cubed + DAMPING_CONST * DAMPING_CONST * DAMPING_CONST)
    velocity = prims[0:3]
    kinetic = velocity[0:1] * velocity[0:1] + velocity[1:2] * velocity[1:2] + velocity[2:3] * velocity[2:3]
    control_volume_heat_level = thermodynamic_stress / fluid_compactness
    visc_left, visc_right = interface_couple(eddy_viscosity)
    interface_molecular_drag = VISCOSITY + 0.5 * (visc_left + visc_right)
    vel_left, vel_right = interface_couple(velocity)
    motion_energy_upwind, motion_energy_downwind = interface_couple(kinetic)
    thermal_state_upwind, thermal_state_downwind = interface_couple(control_volume_heat_level)
    turb_left, turb_right = interface_couple(state[5:6])
    nu_left, nu_right = interface_couple(prims[4:5])
    visc_moment = interface_molecular_drag * (vel_right - vel_left)
    dissipative_heat_flux = interface_molecular_drag * (0.5 * (motion_energy_downwind - motion_energy_upwind) + ADIABATIC_INDEX / ((ADIABATIC_INDEX - 1.0) * DIFFUSIVITY_QUOT) * (thermal_state_downwind - thermal_state_upwind))
    visc_turb = (VISCOSITY + 0.5 * (turb_left + turb_right)) / DIFFUSE_SIGMA * (nu_right - nu_left)
    viscous = jnp.concatenate([jnp.zeros_like(dissipative_heat_flux), visc_moment, dissipative_heat_flux, visc_turb], axis=0)
    return central - damping - viscous

def slope(prims, field, axis):
    cropped = crop_others(prims[field:field + 1], axis)
    count = cropped.shape[axis] - 4
    return 0.5 * (take_slab(cropped, axis, 3, count) - take_slab(cropped, axis, 1, count))

def residual_terms(extended, wide_prims, cell_volume, wall_gap):
    flow = None
    for axis in (1, 2, 3):
        faces = face_flux(extended, wide_prims, axis)
        count = faces.shape[axis] - 1
        term = take_slab(faces, axis, 1, count) - take_slab(faces, axis, 0, count)
        flow = term if flow is None else flow + term
    inner = extended[:, 2:-2, 2:-2, 2:-2]
    spin_first = slope(wide_prims, 2, 2) - slope(wide_prims, 1, 3)
    spin_second = slope(wide_prims, 0, 3) - slope(wide_prims, 2, 1)
    spin_third = slope(wide_prims, 1, 1) - slope(wide_prims, 0, 2)
    spin = jnp.sqrt(jnp.square(spin_first) + jnp.square(spin_second) + jnp.square(spin_third) + 1e-06)
    eddy_field = wide_prims[4:5, 2:-2, 2:-2, 2:-2]
    source = PRODUCE_GAIN * spin * inner[5:6] - DESTROY_GAIN * inner[0:1] * jnp.square(eddy_field / wall_gap[None])
    return jnp.concatenate([flow[:5], flow[5:6] - cell_volume[None] * source], axis=0)

def reference(base_state, section_state, volume, distance, orientation):
    total = GROUPS * CHAIN
    flat = section_state.reshape((total, 6, DEPTH, FACE, FACE))
    base_flat = base_state.reshape((total, 6, DEPTH, FACE, FACE))
    volume_flat = volume.reshape((total, DEPTH, FACE, FACE))
    gap_flat = distance.reshape((total, DEPTH, FACE, FACE))
    flag_flat = orientation.reshape((total, 3))
    blocks = jnp.arange(total, dtype=jnp.int32)

    def block_limit(index):
        block = flat[index]
        return jnp.min(volume_flat[index] / total_speed(block, primitive(block)))
    smallest = jnp.min(lax.map(block_limit, blocks))
    step = COURANT * smallest

    def block_update(index):
        block = flat[index]
        before_index = jnp.maximum(index - 1, 0).astype(jnp.int32)
        after_index = jnp.minimum(index + 1, total - 1).astype(jnp.int32)
        place = index % CHAIN
        extended = assemble(block, flat[before_index][:, DEPTH - 2:], flat[after_index][:, :2], flag_flat[index], flag_flat[after_index], place == 0, place == CHAIN - 1, 2, 3)
        wide_prims = primitive(extended)
        resid = residual_terms(extended, wide_prims, volume_flat[index], gap_flat[index])
        updated = base_flat[index] - SECTION_WEIGHT * step * resid / volume_flat[index][None]
        partial_value = jnp.sum(jnp.square(resid[0] / volume_flat[index]))
        return (updated, partial_value)
    updated, partials = lax.map(block_update, blocks)
    cells = GROUPS * CHAIN * DEPTH * FACE * FACE
    norm = jnp.sqrt(jnp.sum(partials) / cells)
    return (updated.reshape((GROUPS, CHAIN, 6, DEPTH, FACE, FACE)), norm)
```

```python
import functools

import jax
import jax.numpy as jnp
from jax import lax
from jax.experimental import pallas as pl
from jax.experimental.pallas import tpu as pltpu
from jax.sharding import PartitionSpec as P

GAMMA = 1.4
HEAT = 1.4 / (0.4 * 0.72)
CUBE = 7.1 * 7.1 * 7.1
MESH = pl.DeviceIdType.MESH
VMEM = pltpu.VMEM
FACE = 128
PAD = 8


def primitives(w):
    inv = 1.0 / w[0]
    u = [w[1] * inv, w[2] * inv, w[3] * inv]
    kinetic = 0.5 * (w[1] * u[0] + w[2] * u[1] + w[3] * u[2])
    p = 0.4 * (w[4] - kinetic)
    heat = p * inv
    cs = jnp.sqrt(GAMMA * heat)
    chi = w[5] * 20.0
    cubed = chi * chi * chi
    mu = w[5] * cubed / (cubed + CUBE)
    h = 0.5 * (u[0] * u[0] + u[1] * u[1] + u[2] * u[2]) + HEAT * heat
    return {"u": u, "p": p, "cs": cs, "mu": mu, "h": h, "nu": w[5] * inv}


def sensor(before, middle, after):
    twice = 2.0 * middle
    total = after + before
    return jnp.abs(total - twice) / (total + twice)


def face_flux(a, wm, w0, w1, w2, q0, q1, s0, s1, fields=range(6)):
    un0, un1 = q0["u"][a - 1], q1["u"][a - 1]
    half = 0.5 * ((jnp.abs(un0) + q0["cs"]) + (jnp.abs(un1) + q1["cs"]))
    e2 = 0.25 * jnp.maximum(s0, s1)
    e4 = jnp.maximum(0.0, 0.03125 - e2)
    b = half * e4
    c = half * e2 + 3.0 * b
    h0, h1 = 0.5 * un0, 0.5 * un1
    muf = 0.05 + 0.5 * (q0["mu"] + q1["mu"])
    out = []
    for f in fields:
        c0, c1 = w0[f], w1[f]
        if f == 4:
            c0, c1 = c0 + q0["p"], c1 + q1["p"]
        g = c0 * h0 + c1 * h1
        if f == a:
            g = g + 0.5 * (q0["p"] + q1["p"])
        g = g - c * (w1[f] - w0[f]) + b * (w2[f] - wm[f])
        if 1 <= f <= 3:
            g = g - muf * (q1["u"][f - 1] - q0["u"][f - 1])
        elif f == 4:
            g = g - muf * (q1["h"] - q0["h"])
        elif f == 5:
            g = g - (0.075 + 0.75 * (w0[5] + w1[5])) * (q1["nu"] - q0["nu"])
        out.append(g)
    return out


def edge_flux(a, w0, w1, q0, s0):
    un = q0["u"][a - 1]
    b = (jnp.abs(un) + q0["cs"]) * jnp.maximum(0.0, 0.03125 - 0.25 * s0)
    out = []
    for f in range(6):
        c0 = w0[f] + q0["p"] if f == 4 else w0[f]
        g = c0 * un
        if f == a:
            g = g + q0["p"]
        out.append(g + b * (w1[f] - w0[f]))
    return out


NAMES = ("u0", "u1", "u2", "p", "cs", "mu", "h", "nu")


def local_kernel(state, volume, part, vort, limit, wide):
    rows = 8

    for layer in range(2):

        def fill(k, least):
            at = pl.ds(pl.multiple_of(k * rows, rows), rows)
            to = pl.ds(pl.multiple_of(k * rows + PAD, rows), rows)
            w = [state[f, layer, at, :] for f in range(6)]
            q = primitives(w)
            u = q["u"]
            for f in range(6):
                wide[f, layer, to, :] = w[f]
            for i, x in enumerate(u + [q["p"], q["cs"], q["mu"], q["h"], q["nu"]]):
                wide[6 + i, layer, to, :] = x
            speed = (jnp.abs(u[0]) + q["cs"]) + (jnp.abs(u[1]) + q["cs"]) + (jnp.abs(u[2]) + q["cs"])
            return jnp.minimum(least, volume[layer, at, :] / speed)

        start = jnp.full((rows, FACE), jnp.inf, jnp.float32) if layer == 0 else limit[...]
        limit[...] = lax.fori_loop(0, FACE // rows, fill, start)
        for i in range(14):
            head = wide[i, layer, PAD : PAD + 1, :]
            tail = wide[i, layer, PAD + FACE - 1 : PAD + FACE, :]
            wide[i, layer, PAD - 2 : PAD - 1, :] = head
            wide[i, layer, PAD - 1 : PAD, :] = head
            wide[i, layer, PAD + FACE : PAD + FACE + 1, :] = tail
            wide[i, layer, PAD + FACE + 1 : PAD + FACE + 2, :] = tail

    lane = lax.broadcasted_iota(jnp.int32, (rows, FACE), 1)
    row = lax.broadcasted_iota(jnp.int32, (rows, FACE), 0)
    first, last, top = lane == 0, lane == FACE - 1, row == 0

    def after(x):
        return jnp.where(last, x, pltpu.roll(x, FACE - 1, 1))

    def before(x):
        return jnp.where(first, x, pltpu.roll(x, 1, 1))

    for layer in range(2):

        def load(i, k, offset):
            return wide[i, layer, pl.ds(k * rows + PAD + offset, rows), :]

        def cell(k, offset):
            v = [load(6 + i, k, offset) for i in range(8)]
            return {"u": v[:3], "p": v[3], "cs": v[4], "mu": v[5], "h": v[6], "nu": v[7]}

        def states(k, offset):
            return [load(f, k, offset) for f in range(6)]

        def body(k, carry):
            w0, q0 = states(k, 0), cell(k, 0)
            w1, q1 = states(k, 1), cell(k, 1)
            pm, p2 = load(9, k, -1), load(9, k, 2)
            s0 = sensor(pm, q0["p"], q1["p"])
            s1 = sensor(q0["p"], q1["p"], p2)
            g = face_flux(2, states(k, -1), w0, w1, states(k, 2), q0, q1, s0, s1)
            turned = [pltpu.roll(x, 1, 0) for x in g]
            total = [x - jnp.where(top, c, y) for x, y, c in zip(g, turned, carry)]
            d2u0 = 0.5 * (q1["u"][0] - load(6, k, -1))
            d2u2 = 0.5 * (q1["u"][2] - load(8, k, -1))
            w1 = [after(x) for x in w0]
            w2 = [after(x) for x in w1]
            wm = [before(x) for x in w0]
            q1 = {n: after(q0[n]) for n in ("p", "cs", "mu", "h", "nu")}
            q1["u"] = [after(x) for x in q0["u"]]
            s0 = sensor(before(q0["p"]), q0["p"], q1["p"])
            g = face_flux(3, wm, w0, w1, w2, q0, q1, s0, after(s0))
            edge = edge_flux(3, w0, w1, q0, s0)
            total = [
                t + (x - jnp.where(first, e, pltpu.roll(x, 1, 1)))
                for t, x, e in zip(total, g, edge)
            ]
            d3u0 = 0.5 * (q1["u"][0] - before(q0["u"][0]))
            d3u1 = 0.5 * (q1["u"][1] - before(q0["u"][1]))
            at = pl.ds(pl.multiple_of(k * rows, rows), rows)
            for f in range(6):
                part[f, layer, at, :] = total[f]
            vort[0, layer, at, :] = d2u2 - d3u1
            vort[1, layer, at, :] = d3u0
            vort[2, layer, at, :] = d2u0
            return tuple(turned)

        w0, q0 = states(0, 0), cell(0, 0)
        p1 = load(9, 0, 1)
        init = edge_flux(2, w0, states(0, 1), q0, sensor(load(9, 0, -1), q0["p"], p1))
        lax.fori_loop(0, FACE // rows, body, tuple(init))


def chain_kernel(
    flags, least, state, base, volume, distance, part, vort, below, above, new, acc, low, high
):
    rows = 8
    steps = FACE // rows
    lane = lax.broadcasted_iota(jnp.int32, (rows, FACE), 1)
    row = lax.broadcasted_iota(jnp.int32, (rows, FACE), 0)

    def ghosts(source, target, turn, flip_rows, flip_lanes, sign2, sign3):
        lanes = jnp.where(flip_lanes > 0, FACE - 1 - lane, lane)
        rowi = jnp.where(flip_rows > 0, rows - 1 - row, row)

        def place(read):
            def body(k, _):
                kk = jnp.where(flip_rows > 0, steps - 1 - k, k)
                at = pl.ds(pl.multiple_of(kk * rows, rows), rows)
                to = pl.ds(pl.multiple_of(k * rows, rows), rows)
                for f in range(6):
                    for layer in range(2):
                        x = read(f, layer, at)
                        x = jnp.take_along_axis(x, lanes, axis=1)
                        x = jnp.take_along_axis(x, rowi, axis=0)
                        if f == 2:
                            x = x * sign2
                        if f == 3:
                            x = x * sign3
                        target[f, layer, to, :] = x
                return 0

            lax.fori_loop(0, steps, body, 0)

        @pl.when(turn > 0)
        def _():
            for f in range(6):
                g = {2: 3, 3: 2}.get(f, f)
                for layer in range(2):
                    new[f, layer] = source[g, layer].T
            place(lambda f, layer, at: new[f, layer, at, :])

        @pl.when(turn == 0)
        def _():
            place(lambda f, layer, at: source[f, layer, at, :])

    is_first, is_last = flags[6], flags[7]

    @pl.when(is_first > 0)
    def _():
        for f in range(6):
            for layer in range(2):
                low[f, layer] = state[f, 0]

    @pl.when(is_first == 0)
    def _():
        t, r2, r3 = flags[0], flags[1], flags[2]
        s2 = 1.0 - 2.0 * jnp.where(t > 0, r3, r2).astype(jnp.float32)
        s3 = 1.0 - 2.0 * jnp.where(t > 0, r2, r3).astype(jnp.float32)
        ghosts(below, low, t, jnp.where(t > 0, r3, r2), jnp.where(t > 0, r2, r3), s2, s3)

    @pl.when(is_last > 0)
    def _():
        for f in range(6):
            for layer in range(2):
                high[f, layer] = state[f, 1]

    @pl.when(is_last == 0)
    def _():
        t, r2, r3 = flags[3], flags[4], flags[5]
        s2 = 1.0 - 2.0 * r2.astype(jnp.float32)
        s3 = 1.0 - 2.0 * r3.astype(jnp.float32)
        ghosts(above, high, t, r2, r3, s2, s3)

    smallest = least[0, 0]

    def body(k, total):
        at = pl.ds(pl.multiple_of(k * rows, rows), rows)
        w = []
        for ref, layer in ((low, 0), (low, 1), (state, 0), (state, 1), (high, 0), (high, 1)):
            w.append([ref[f, layer, at, :] for f in range(6)])
        q = [primitives(x) for x in w]
        s = [None] + [sensor(q[i - 1]["p"], q[i]["p"], q[i + 1]["p"]) for i in range(1, 5)]
        g = [
            face_flux(1, w[i - 1], w[i], w[i + 1], w[i + 2], q[i], q[i + 1], s[i], s[i + 1])
            for i in range(1, 4)
        ]
        for layer in range(2):
            i = layer + 2
            vol = volume[layer, at, :]
            inv = 1.0 / vol
            scale = smallest * inv
            d1u1 = 0.5 * (q[i + 1]["u"][1] - q[i - 1]["u"][1])
            d1u2 = 0.5 * (q[i + 1]["u"][2] - q[i - 1]["u"][2])
            w1 = vort[0, layer, at, :]
            w2 = vort[1, layer, at, :] - d1u2
            w3 = d1u1 - vort[2, layer, at, :]
            spin = jnp.sqrt(w1 * w1 + w2 * w2 + w3 * w3 + 1e-6)
            ratio = q[i]["nu"] / distance[layer, at, :]
            source = 0.1355 * spin * w[i][5] - 3.239 * w[i][0] * (ratio * ratio)
            for f in range(6):
                r = part[f, layer, at, :] + (g[layer + 1][f] - g[layer][f])
                if f == 5:
                    r = r - vol * source
                if f == 0:
                    z = r * inv
                    total = total + z * z
                new[f, layer, at, :] = base[f, layer, at, :] - scale * r
        return total

    acc[...] = lax.fori_loop(0, steps, body, jnp.zeros((rows, FACE), jnp.float32))


def reduce_kernel(op, value, out, slots, send, recv):
    comp, blk = lax.axis_index("comp"), lax.axis_index("blk")
    low, high = blk % 8, blk // 8
    phases = (
        (low, lambda j: (comp, high * 8 + j)),
        (comp, lambda j: (j, blk)),
        (high, lambda j: (comp, j * 8 + low)),
    )
    barrier = pltpu.get_barrier_semaphore()
    for me, device in phases:
        for step in range(1, 8):
            pl.semaphore_signal(
                barrier, inc=1, device_id=device((me + step) % 8), device_id_type=MESH
            )
    pl.semaphore_wait(barrier, 21)
    held = value[...]
    for n, (me, device) in enumerate(phases):
        slots[n, pl.ds(me, 1)] = held[None]
        copies = []
        for step in range(1, 8):
            copy = pltpu.make_async_remote_copy(
                src_ref=slots.at[n, me],
                dst_ref=slots.at[n, me],
                send_sem=send.at[n, step],
                recv_sem=recv.at[n, me],
                device_id=device((me + step) % 8),
                device_id_type=MESH,
            )
            copy.start()
            copies.append(copy)
        for step in range(1, 8):
            other = (me + step) % 8
            pltpu.make_async_remote_copy(
                src_ref=slots.at[n, me],
                dst_ref=slots.at[n, other],
                send_sem=send.at[n, step],
                recv_sem=recv.at[n, other],
                device_id=device(other),
                device_id_type=MESH,
            ).wait_recv()
        held = slots[n, 0]
        for j in range(1, 8):
            held = jnp.minimum(held, slots[n, j]) if op == "min" else held + slots[n, j]
        for copy in copies:
            copy.wait_send()
    if op == "min":
        out[...] = jnp.min(held, axis=(0, 1), keepdims=True)
    else:
        out[...] = jnp.sum(held, axis=(0, 1), keepdims=True)


def reduce_all(op, value, collective_id):
    return pl.pallas_call(
        functools.partial(reduce_kernel, op),
        out_shape=jax.ShapeDtypeStruct((1, 1), jnp.float32),
        in_specs=[pl.BlockSpec(memory_space=VMEM)],
        out_specs=pl.BlockSpec(memory_space=VMEM),
        scratch_shapes=[
            VMEM((3, 8, 8, FACE), jnp.float32),
            pltpu.SemaphoreType.DMA((3, 8)),
            pltpu.SemaphoreType.DMA((3, 8)),
        ],
        compiler_params=pltpu.CompilerParams(collective_id=collective_id, has_side_effects=True),
        cost_estimate=pl.CostEstimate(flops=1000, bytes_accessed=2**20, transcendentals=0),
        name="reduce_" + op,
    )(value)


def per_device(base_state, section_state, volume, distance, orientation):
    state, base = section_state[0, 0], base_state[0, 0]
    vol, gap = volume[0, 0], distance[0, 0]
    group, place = lax.axis_index("comp"), lax.axis_index("blk")
    chain = lax.axis_size("blk")
    f32 = functools.partial(jax.ShapeDtypeStruct, dtype=jnp.float32)
    vm = pl.BlockSpec(memory_space=VMEM)
    sm = pl.BlockSpec(memory_space=pltpu.SMEM)
    plane = (2, FACE, FACE)

    below = lax.ppermute(state, "blk", [(i, i + 1) for i in range(chain - 1)])
    above = lax.ppermute(state, "blk", [(i + 1, i) for i in range(chain - 1)])

    part, vort, limit = pl.pallas_call(
        local_kernel,
        out_shape=(f32((6,) + plane), f32((3,) + plane), f32((8, FACE))),
        in_specs=[vm, vm],
        out_specs=(vm, vm, vm),
        scratch_shapes=[VMEM((14, 2, FACE + 2 * PAD, FACE), jnp.float32)],
        cost_estimate=pl.CostEstimate(
            flops=40_000_000, bytes_accessed=3_000_000, transcendentals=400_000
        ),
        name="local_flux",
    )(state, vol)
    least = reduce_all("min", limit, 1)

    table = lax.dynamic_index_in_dim(orientation, group, 0, keepdims=False)
    mine = lax.dynamic_index_in_dim(table, place, 0, keepdims=False)
    after = lax.dynamic_index_in_dim(table, jnp.minimum(place + 1, chain - 1), 0, keepdims=False)
    ends = jnp.stack([place == 0, place == chain - 1]).astype(jnp.int32)
    flags = jnp.concatenate([mine, after, ends])

    new, acc = pl.pallas_call(
        chain_kernel,
        out_shape=(f32((6,) + plane), f32((8, FACE))),
        in_specs=[sm, sm] + [vm] * 8,
        out_specs=(vm, vm),
        scratch_shapes=[VMEM((6,) + plane, jnp.float32)] * 2,
        cost_estimate=pl.CostEstimate(
            flops=40_000_000, bytes_accessed=5_000_000, transcendentals=400_000
        ),
        name="chain_flux",
    )(flags, least, state, base, vol, gap, part, vort, below, above)
    total = reduce_all("sum", acc, 2)
    cells = lax.axis_size("comp") * chain * 2 * FACE * FACE
    return new[None, None], jnp.sqrt(total[0, 0] / cells)


def solution(mesh):
    wide = P("comp", "blk", None, None, None, None)
    cell = P("comp", "blk", None, None, None)
    return jax.shard_map(
        per_device,
        mesh=mesh,
        in_specs=(wide, wide, cell, cell, P()),
        out_specs=(wide, P()),
        check_vma=False,
    )
```

```python
import functools

import jax
import jax.numpy as jnp
from jax import lax
from jax.experimental import pallas as pl
from jax.experimental.pallas import tpu as pltpu
from jax.sharding import PartitionSpec as P

GAMMA = 1.4
HEAT = 1.4 / (0.4 * 0.72)
CUBE = 7.1 * 7.1 * 7.1
MESH = pl.DeviceIdType.MESH
VMEM = pltpu.VMEM
FACE = 128
PAD = 8


def primitives(w):
    inv = 1.0 / w[0]
    u = [w[1] * inv, w[2] * inv, w[3] * inv]
    kinetic = 0.5 * (w[1] * u[0] + w[2] * u[1] + w[3] * u[2])
    p = 0.4 * (w[4] - kinetic)
    heat = p * inv
    cs = jnp.sqrt(GAMMA * heat)
    chi = w[5] * 20.0
    cubed = chi * chi * chi
    mu = w[5] * cubed / (cubed + CUBE)
    h = 0.5 * (u[0] * u[0] + u[1] * u[1] + u[2] * u[2]) + HEAT * heat
    return {"u": u, "p": p, "cs": cs, "mu": mu, "h": h, "nu": w[5] * inv}


def sensor(before, middle, after):
    twice = 2.0 * middle
    total = after + before
    return jnp.abs(total - twice) / (total + twice)


def face_flux(a, wm, w0, w1, w2, q0, q1, s0, s1, fields=range(6)):
    un0, un1 = q0["u"][a - 1], q1["u"][a - 1]
    half = 0.5 * ((jnp.abs(un0) + q0["cs"]) + (jnp.abs(un1) + q1["cs"]))
    e2 = 0.25 * jnp.maximum(s0, s1)
    e4 = jnp.maximum(0.0, 0.03125 - e2)
    b = half * e4
    c = half * e2 + 3.0 * b
    h0, h1 = 0.5 * un0, 0.5 * un1
    muf = 0.05 + 0.5 * (q0["mu"] + q1["mu"])
    out = []
    for f in fields:
        c0, c1 = w0[f], w1[f]
        if f == 4:
            c0, c1 = c0 + q0["p"], c1 + q1["p"]
        g = c0 * h0 + c1 * h1
        if f == a:
            g = g + 0.5 * (q0["p"] + q1["p"])
        g = g - c * (w1[f] - w0[f]) + b * (w2[f] - wm[f])
        if 1 <= f <= 3:
            g = g - muf * (q1["u"][f - 1] - q0["u"][f - 1])
        elif f == 4:
            g = g - muf * (q1["h"] - q0["h"])
        elif f == 5:
            g = g - (0.075 + 0.75 * (w0[5] + w1[5])) * (q1["nu"] - q0["nu"])
        out.append(g)
    return out


def edge_flux(a, w0, w1, q0, s0):
    un = q0["u"][a - 1]
    b = (jnp.abs(un) + q0["cs"]) * jnp.maximum(0.0, 0.03125 - 0.25 * s0)
    out = []
    for f in range(6):
        c0 = w0[f] + q0["p"] if f == 4 else w0[f]
        g = c0 * un
        if f == a:
            g = g + q0["p"]
        out.append(g + b * (w1[f] - w0[f]))
    return out


ROWS = 8
STEPS = FACE // ROWS
ORDER = ((2, 3), (0,), (1,), (4,), (5,))


def kernel(refs):
    comp, blk = lax.axis_index("comp"), lax.axis_index("blk")
    chain = lax.axis_size("blk")
    flags, state_hbm, volume_hbm, distance_hbm = refs["inputs"]
    change_hbm, least_out, total_out = refs["outputs"]
    state, volume, distance = refs["state"], refs["volume"], refs["distance"]
    wide, part, vort, change = refs["wide"], refs["part"], refs["vort"], refs["change"]
    ghost, slots = refs["ghost"], refs["slots"]
    halo = (refs["halo"][:6], refs["halo"][6:])
    load_sem, hsend, hrecv, rsend, rrecv = refs["sems"]

    low, high = blk % 8, blk // 8
    phases = (
        (low, lambda j: (comp, high * 8 + j)),
        (comp, lambda j: (j, blk)),
        (high, lambda j: (comp, j * 8 + low)),
    )
    has_below, has_above = blk > 0, blk < chain - 1
    below_id = (comp, jnp.maximum(blk - 1, 0))
    above_id = (comp, jnp.minimum(blk + 1, chain - 1))

    barrier = pltpu.get_barrier_semaphore()
    for has, device in ((has_below, below_id), (has_above, above_id)):

        @pl.when(has)
        def _():
            pl.semaphore_signal(barrier, inc=1, device_id=device, device_id_type=MESH)

    for me, device in phases:
        for step in range(1, 8):
            pl.semaphore_signal(
                barrier, inc=1, device_id=device((me + step) % 8), device_id_type=MESH
            )

    loads = [
        pltpu.make_async_copy(state_hbm, state, load_sem.at[0]),
        pltpu.make_async_copy(volume_hbm, volume, load_sem.at[1]),
        pltpu.make_async_copy(distance_hbm, distance, load_sem.at[2]),
    ]
    for copy in loads:
        copy.start()
    for copy in loads:
        copy.wait()

    def rows_of(k):
        return pl.ds(pl.multiple_of(k * ROWS, ROWS), ROWS)

    def fill(k, least):
        at = rows_of(k)
        to = pl.ds(pl.multiple_of(k * ROWS + PAD, ROWS), ROWS)
        for layer in range(2):
            w = [state[f, layer, at, :] for f in range(6)]
            q = primitives(w)
            u = q["u"]
            for f in range(6):
                wide[f, layer, to, :] = w[f]
            for i, x in enumerate(u + [q["p"], q["cs"], q["mu"], q["h"], q["nu"]]):
                wide[6 + i, layer, to, :] = x
            speed = (jnp.abs(u[0]) + q["cs"]) + (jnp.abs(u[1]) + q["cs"]) + (jnp.abs(u[2]) + q["cs"])
            least = jnp.minimum(least, volume[layer, at, :] / speed)
        return least

    limit = lax.fori_loop(0, STEPS, fill, jnp.full((ROWS, FACE), jnp.inf, jnp.float32))
    for layer in range(2):
        for i in range(14):
            first_row = wide[i, layer, PAD : PAD + 1, :]
            last_row = wide[i, layer, PAD + FACE - 1 : PAD + FACE, :]
            wide[i, layer, PAD - 2 : PAD - 1, :] = first_row
            wide[i, layer, PAD - 1 : PAD, :] = first_row
            wide[i, layer, PAD + FACE : PAD + FACE + 1, :] = last_row
            wide[i, layer, PAD + FACE + 1 : PAD + FACE + 2, :] = last_row

    pl.semaphore_wait(
        barrier, 21 + has_below.astype(jnp.int32) + has_above.astype(jnp.int32)
    )

    def exchange(kind, n, step):
        me, device = phases[n]
        return pltpu.make_async_remote_copy(
            src_ref=slots.at[kind, n, me],
            dst_ref=slots.at[kind, n, me],
            send_sem=rsend.at[kind, n, step],
            recv_sem=rrecv.at[kind, n, me],
            device_id=device((me + step) % 8),
            device_id_type=MESH,
        )

    def send(kind, n, value):
        slots[kind, n, pl.ds(phases[n][0], 1)] = value[None]
        for step in range(1, 8):
            exchange(kind, n, step).start()

    def receive(kind, n, op):
        me, device = phases[n]
        for step in range(1, 8):
            other = (me + step) % 8
            pltpu.make_async_remote_copy(
                src_ref=slots.at[kind, n, me],
                dst_ref=slots.at[kind, n, other],
                send_sem=rsend.at[kind, n, step],
                recv_sem=rrecv.at[kind, n, other],
                device_id=device(other),
                device_id_type=MESH,
            ).wait_recv()
        held = slots[kind, n, 0]
        for j in range(1, 8):
            held = op(held, slots[kind, n, j])
        for step in range(1, 8):
            exchange(kind, n, step).wait_send()
        return held

    send(0, 0, limit)

    sides = ((has_below, has_above, above_id), (has_above, has_below, below_id))

    def halo_copy(side, f):
        return pltpu.make_async_remote_copy(
            src_ref=state_hbm.at[f],
            dst_ref=halo[side][f].at[0],
            send_sem=hsend.at[side, f],
            recv_sem=hrecv.at[side, f],
            device_id=sides[side][2],
            device_id_type=MESH,
        )

    for fields in ORDER:
        for f in fields:
            for side in range(2):

                @pl.when(sides[side][1])
                def _():
                    halo_copy(side, f).start()

    lane = lax.broadcasted_iota(jnp.int32, (ROWS, FACE), 1)
    row = lax.broadcasted_iota(jnp.int32, (ROWS, FACE), 0)
    first, last, top = lane == 0, lane == FACE - 1, row == 0

    def after(x):
        return jnp.where(last, x, pltpu.roll(x, FACE - 1, 1))

    def before(x):
        return jnp.where(first, x, pltpu.roll(x, 1, 1))

    def local_flux(layer):
        def load(i, k, offset):
            return wide[i, layer, pl.ds(k * ROWS + PAD + offset, ROWS), :]

        def cell(k, offset):
            v = [load(6 + i, k, offset) for i in range(8)]
            return {"u": v[:3], "p": v[3], "cs": v[4], "mu": v[5], "h": v[6], "nu": v[7]}

        def states(k, offset):
            return [load(f, k, offset) for f in range(6)]

        def body(k, carry):
            w0, q0 = states(k, 0), cell(k, 0)
            w1, q1 = states(k, 1), cell(k, 1)
            pm, p2 = load(9, k, -1), load(9, k, 2)
            s0 = sensor(pm, q0["p"], q1["p"])
            s1 = sensor(q0["p"], q1["p"], p2)
            g = face_flux(2, states(k, -1), w0, w1, states(k, 2), q0, q1, s0, s1)
            turned = [pltpu.roll(x, 1, 0) for x in g]
            total = [x - jnp.where(top, c, y) for x, y, c in zip(g, turned, carry)]
            d2u0 = 0.5 * (q1["u"][0] - load(6, k, -1))
            d2u2 = 0.5 * (q1["u"][2] - load(8, k, -1))
            w1 = [after(x) for x in w0]
            w2 = [after(x) for x in w1]
            wm = [before(x) for x in w0]
            q1 = {n: after(q0[n]) for n in ("p", "cs", "mu", "h", "nu")}
            q1["u"] = [after(x) for x in q0["u"]]
            s0 = sensor(before(q0["p"]), q0["p"], q1["p"])
            g = face_flux(3, wm, w0, w1, w2, q0, q1, s0, after(s0))
            edge = edge_flux(3, w0, w1, q0, s0)
            total = [
                t + (x - jnp.where(first, e, pltpu.roll(x, 1, 1)))
                for t, x, e in zip(total, g, edge)
            ]
            d3u0 = 0.5 * (q1["u"][0] - before(q0["u"][0]))
            d3u1 = 0.5 * (q1["u"][1] - before(q0["u"][1]))
            at = rows_of(k)
            for f in range(6):
                part[f, layer, at, :] = total[f]
            vort[0, layer, at, :] = d2u2 - d3u1
            vort[1, layer, at, :] = d3u0
            vort[2, layer, at, :] = d2u0
            return tuple(turned)

        w0, q0 = states(0, 0), cell(0, 0)
        p1 = load(9, 0, 1)
        init = edge_flux(2, w0, states(0, 1), q0, sensor(load(9, 0, -1), q0["p"], p1))
        lax.fori_loop(0, STEPS, body, tuple(init))

    local_flux(0)
    send(0, 1, receive(0, 0, jnp.minimum))
    local_flux(1)
    send(0, 2, receive(0, 1, jnp.minimum))

    def one_if(condition):
        return jnp.where(condition, 1, 0)

    up = jnp.minimum(blk + 1, chain - 1)
    t, r2, r3 = [flags[i, comp, blk] * one_if(has_below) for i in range(3)]
    lower = (t, t * r3 + (1 - t) * r2, t * r2 + (1 - t) * r3)
    upper = tuple(flags[i, comp, up] * one_if(has_above) for i in range(3))

    for fields in ORDER:
        for side, (t, flip_rows, flip_lanes) in enumerate((lower, upper)):
            buf = halo[side]
            for f in fields:

                @pl.when(sides[side][0])
                def _():
                    halo_copy(side, f).wait_recv()

                @pl.when(jnp.logical_not(sides[side][0]))
                def _():
                    for layer in range(2):
                        buf[f][0, layer] = state[f, side]

            for f in fields:
                for layer in range(2):
                    buf[f][1, layer] = buf[{2: 3, 3: 2}.get(f, f)][0, layer].T
            turn, reverse_rows, reverse_lanes = [
                jnp.broadcast_to(x, (ROWS, FACE)) > 0 for x in (t, flip_rows, flip_lanes)
            ]
            signs = {
                2: 1.0 - 2.0 * flip_rows.astype(jnp.float32),
                3: 1.0 - 2.0 * flip_lanes.astype(jnp.float32),
            }

            def place(k, _):
                pair = (rows_of(k), rows_of(STEPS - 1 - k))
                for f in fields:
                    for layer in range(2):
                        x = [
                            jnp.where(turn, buf[f][1, layer, at, :], buf[f][0, layer, at, :])
                            for at in pair
                        ]
                        flipped = [jnp.take_along_axis(y, ROWS - 1 - row, axis=0) for y in x]
                        for i in range(2):
                            y = jnp.where(reverse_rows, flipped[1 - i], x[i])
                            z = jnp.take_along_axis(y, FACE - 1 - lane, axis=1)
                            y = jnp.where(reverse_lanes, z, y)
                            if f in signs:
                                y = y * signs[f]
                            ghost[side, f, layer, pair[i], :] = y
                return 0

            lax.fori_loop(0, STEPS // 2, place, 0)

    least = receive(0, 2, jnp.minimum)
    least_out[...] = jnp.min(least, axis=(0, 1), keepdims=True)

    def own(i, layer, k):
        return wide[i, layer, pl.ds(pl.multiple_of(k * ROWS + PAD, ROWS), ROWS), :]

    def density(k, total):
        at = rows_of(k)
        rho, p, un, cs = [], [], [], []
        for side, layer in ((0, 0), (0, 1), (None, 0), (None, 1), (1, 0), (1, 1)):
            if side is None:
                rho.append(own(0, layer, k))
                un.append(own(6, layer, k))
                p.append(own(9, layer, k))
                cs.append(own(10, layer, k))
            else:
                w = [ghost[side, f, layer, at, :] for f in range(5)]
                q = primitives(w + [w[0]])
                rho.append(w[0])
                un.append(q["u"][0])
                p.append(q["p"])
                cs.append(q["cs"])
        s = [None] + [sensor(p[i - 1], p[i], p[i + 1]) for i in range(1, 5)]
        g = []
        for i in range(1, 4):
            half = 0.5 * ((jnp.abs(un[i]) + cs[i]) + (jnp.abs(un[i + 1]) + cs[i + 1]))
            e2 = 0.25 * jnp.maximum(s[i], s[i + 1])
            b = half * jnp.maximum(0.0, 0.03125 - e2)
            c = half * e2 + 3.0 * b
            g.append(
                0.5 * (rho[i] * un[i] + rho[i + 1] * un[i + 1])
                - c * (rho[i + 1] - rho[i])
                + b * (rho[i + 2] - rho[i - 1])
            )
        for layer in range(2):
            z = (part[0, layer, at, :] + (g[layer + 1] - g[layer])) / volume[layer, at, :]
            change[0, layer, at, :] = z
            total = total + z * z
        return total

    total = lax.fori_loop(0, STEPS, density, jnp.zeros((ROWS, FACE), jnp.float32))
    send(1, 0, total)

    def rest(k, _):
        at = rows_of(k)
        w, q = [], []
        for side, layer in ((0, 0), (0, 1), (None, 0), (None, 1), (1, 0), (1, 1)):
            if side is None:
                w.append([own(f, layer, k) for f in range(6)])
                v = [own(6 + i, layer, k) for i in range(8)]
                q.append({"u": v[:3], "p": v[3], "cs": v[4], "mu": v[5], "h": v[6], "nu": v[7]})
            else:
                w.append([ghost[side, f, layer, at, :] for f in range(6)])
                q.append(primitives(w[-1]))
        s = [None] + [sensor(q[i - 1]["p"], q[i]["p"], q[i + 1]["p"]) for i in range(1, 5)]
        fields = range(1, 6)
        g = [
            face_flux(1, w[i - 1], w[i], w[i + 1], w[i + 2], q[i], q[i + 1], s[i], s[i + 1], fields)
            for i in range(1, 4)
        ]
        for layer in range(2):
            i = layer + 2
            vol = volume[layer, at, :]
            inv = 1.0 / vol
            d1u1 = 0.5 * (q[i + 1]["u"][1] - q[i - 1]["u"][1])
            d1u2 = 0.5 * (q[i + 1]["u"][2] - q[i - 1]["u"][2])
            w1 = vort[0, layer, at, :]
            w2 = vort[1, layer, at, :] - d1u2
            w3 = d1u1 - vort[2, layer, at, :]
            spin = jnp.sqrt(w1 * w1 + w2 * w2 + w3 * w3 + 1e-6)
            ratio = q[i]["nu"] / distance[layer, at, :]
            source = 0.1355 * spin * w[i][5] - 3.239 * w[i][0] * (ratio * ratio)
            for f in fields:
                r = part[f, layer, at, :] + (g[layer + 1][f - 1] - g[layer][f - 1])
                if f == 5:
                    r = r - vol * source
                change[f, layer, at, :] = r * inv
        return 0

    lax.fori_loop(0, 6, rest, 0)
    send(1, 1, receive(1, 0, jnp.add))
    lax.fori_loop(6, STEPS, rest, 0)
    store = pltpu.make_async_copy(change, change_hbm, load_sem.at[3])
    store.start()
    send(1, 2, receive(1, 1, jnp.add))
    for side in range(2):
        for f in range(6):

            @pl.when(sides[side][1])
            def _():
                halo_copy(side, f).wait_send()

    total_out[...] = jnp.sum(receive(1, 2, jnp.add), axis=(0, 1), keepdims=True)
    store.wait()


def entry(*args):
    names = ("state", "volume", "distance", "wide", "part", "vort", "change", "ghost", "slots")
    refs = {"inputs": args[:4], "outputs": args[4:7]}
    refs.update(zip(names, args[7:16]))
    refs["halo"] = args[16:28]
    refs["sems"] = args[28:]
    kernel(refs)


def per_device(base_state, section_state, volume, distance, orientation):
    f32 = functools.partial(jax.ShapeDtypeStruct, dtype=jnp.float32)
    scratch = functools.partial(VMEM, dtype=jnp.float32)
    hbm = pl.BlockSpec(memory_space=pl.ANY)
    vm = pl.BlockSpec(memory_space=VMEM)
    plane = (2, FACE, FACE)
    dma = pltpu.SemaphoreType.DMA
    change, least, total = pl.pallas_call(
        entry,
        out_shape=(f32((6,) + plane), f32((1, 1)), f32((1, 1))),
        in_specs=[pl.BlockSpec(memory_space=pltpu.SMEM), hbm, hbm, hbm],
        out_specs=(hbm, vm, vm),
        scratch_shapes=[
            scratch((6,) + plane),
            scratch(plane),
            scratch(plane),
            scratch((14, 2, FACE + 2 * PAD, FACE)),
            scratch((6,) + plane),
            scratch((3,) + plane),
            scratch((6,) + plane),
            scratch((2, 6) + plane),
            scratch((2, 3, 8, 8, FACE)),
        ]
        + [scratch((2,) + plane)] * 12
        + [dma((4,)), dma((2, 6)), dma((2, 6)), dma((2, 3, 8)), dma((2, 3, 8))],
        compiler_params=pltpu.CompilerParams(collective_id=1, has_side_effects=True),
        cost_estimate=pl.CostEstimate(
            flops=80_000_000, bytes_accessed=4_000_000, transcendentals=800_000
        ),
        name="section",
    )(jnp.transpose(orientation, (2, 0, 1)), section_state[0, 0], volume[0, 0], distance[0, 0])
    new = base_state[0, 0] - least[0, 0] * change
    cells = lax.axis_size("comp") * lax.axis_size("blk") * 2 * FACE * FACE
    return new[None, None], jnp.sqrt(total[0, 0] / cells)


def solution(mesh):
    wide = P("comp", "blk", None, None, None, None)
    cell = P("comp", "blk", None, None, None)
    return jax.shard_map(
        per_device,
        mesh=mesh,
        in_specs=(wide, wide, cell, cell, P()),
        out_specs=(wide, P()),
        check_vma=False,
    )
```

```python
import functools

import jax
import jax.numpy as jnp
from jax import lax
from jax.experimental import pallas as pl
from jax.experimental.pallas import tpu as pltpu
from jax.sharding import PartitionSpec as P

GAMMA = 1.4
HEAT = 1.4 / (0.4 * 0.72)
CUBE = 7.1 * 7.1 * 7.1
MESH = pl.DeviceIdType.MESH
VMEM = pltpu.VMEM
FACE = 128
PAD = 8


def primitives(w):
    inv = 1.0 / w[0]
    u = [w[1] * inv, w[2] * inv, w[3] * inv]
    kinetic = 0.5 * (w[1] * u[0] + w[2] * u[1] + w[3] * u[2])
    p = 0.4 * (w[4] - kinetic)
    heat = p * inv
    cs = jnp.sqrt(GAMMA * heat)
    chi = w[5] * 20.0
    cubed = chi * chi * chi
    mu = w[5] * cubed / (cubed + CUBE)
    h = 0.5 * (u[0] * u[0] + u[1] * u[1] + u[2] * u[2]) + HEAT * heat
    return {"u": u, "p": p, "cs": cs, "mu": mu, "h": h, "nu": w[5] * inv}


def sensor(before, middle, after):
    twice = 2.0 * middle
    total = after + before
    return jnp.abs(total - twice) / (total + twice)


def face_flux(a, wm, w0, w1, w2, q0, q1, s0, s1, fields=range(6)):
    un0, un1 = q0["u"][a - 1], q1["u"][a - 1]
    half = 0.5 * ((jnp.abs(un0) + q0["cs"]) + (jnp.abs(un1) + q1["cs"]))
    e2 = 0.25 * jnp.maximum(s0, s1)
    e4 = jnp.maximum(0.0, 0.03125 - e2)
    b = half * e4
    c = half * e2 + 3.0 * b
    h0, h1 = 0.5 * un0, 0.5 * un1
    muf = 0.05 + 0.5 * (q0["mu"] + q1["mu"])
    out = []
    for f in fields:
        c0, c1 = w0[f], w1[f]
        if f == 4:
            c0, c1 = c0 + q0["p"], c1 + q1["p"]
        g = c0 * h0 + c1 * h1
        if f == a:
            g = g + 0.5 * (q0["p"] + q1["p"])
        g = g - c * (w1[f] - w0[f]) + b * (w2[f] - wm[f])
        if 1 <= f <= 3:
            g = g - muf * (q1["u"][f - 1] - q0["u"][f - 1])
        elif f == 4:
            g = g - muf * (q1["h"] - q0["h"])
        elif f == 5:
            g = g - (0.075 + 0.75 * (w0[5] + w1[5])) * (q1["nu"] - q0["nu"])
        out.append(g)
    return out


def edge_flux(a, w0, w1, q0, s0, fields=range(6)):
    un = q0["u"][a - 1]
    b = (jnp.abs(un) + q0["cs"]) * jnp.maximum(0.0, 0.03125 - 0.25 * s0)
    out = []
    for f in fields:
        c0 = w0[f] + q0["p"] if f == 4 else w0[f]
        g = c0 * un
        if f == a:
            g = g + q0["p"]
        out.append(g + b * (w1[f] - w0[f]))
    return out


ROWS = 8
STEPS = FACE // ROWS
ORDER = ((2, 3), (0,), (1,), (4,), (5,))


def kernel(refs):
    comp, blk = lax.axis_index("comp"), lax.axis_index("blk")
    chain = lax.axis_size("blk")
    flags_hbm, state_hbm, volume_hbm, distance_hbm, base_hbm = refs["inputs"]
    new_hbm, total_out = refs["outputs"]
    flags, base = refs["flags"], refs["base"]
    state, volume, distance = refs["state"], refs["volume"], refs["distance"]
    wide, part, vort, change = refs["wide"], refs["part"], refs["vort"], refs["change"]
    ghost, slots = refs["ghost"], refs["slots"]
    halo = (refs["halo"][:6], refs["halo"][6:])
    load_sem, hsend, hrecv, rsend, rrecv = refs["sems"]

    low, high = blk % 8, blk // 8
    phases = (
        (low, lambda j: (comp, high * 8 + j)),
        (comp, lambda j: (j, blk)),
        (high, lambda j: (comp, j * 8 + low)),
    )
    has_below, has_above = blk > 0, blk < chain - 1
    below_id = (comp, jnp.maximum(blk - 1, 0))
    above_id = (comp, jnp.minimum(blk + 1, chain - 1))

    loads = [
        pltpu.make_async_copy(source, target, load_sem.at[i])
        for i, (source, target) in enumerate(
            (
                (state_hbm, state),
                (volume_hbm, volume),
                (flags_hbm, flags),
                (distance_hbm, distance),
                (base_hbm, base),
            )
        )
    ]
    for copy in loads:
        copy.start()

    barrier = pltpu.get_barrier_semaphore()
    for has, device in ((has_below, below_id), (has_above, above_id)):

        @pl.when(has)
        def _():
            pl.semaphore_signal(barrier, inc=1, device_id=device, device_id_type=MESH)

    for me, device in phases:
        for step in range(1, 8):
            pl.semaphore_signal(
                barrier, inc=1, device_id=device((me + step) % 8), device_id_type=MESH
            )

    def rows_of(k):
        return pl.ds(pl.multiple_of(k * ROWS, ROWS), ROWS)

    loads[0].wait()
    loads[1].wait()

    def fill_rows(k, least):
        at = rows_of(k)
        to = pl.ds(pl.multiple_of(k * ROWS + PAD, ROWS), ROWS)
        for layer in range(2):
            w = [state[f, layer, at, :] for f in range(6)]
            q = primitives(w)
            u = q["u"]
            for f in range(6):
                wide[f, layer, to, :] = w[f]
            for i, x in enumerate(u + [q["p"], q["cs"], q["mu"], q["h"], q["nu"]]):
                wide[6 + i, layer, to, :] = x
            speed = (jnp.abs(u[0]) + q["cs"]) + (jnp.abs(u[1]) + q["cs"]) + (jnp.abs(u[2]) + q["cs"])
            least = jnp.minimum(least, volume[layer, at, :] / speed)
        return least

    def fill(k, least):
        return fill_rows(2 * k + 1, fill_rows(2 * k, least))

    limit = lax.fori_loop(0, STEPS // 2, fill, jnp.full((ROWS, FACE), jnp.inf, jnp.float32))
    for layer in range(2):
        for i in range(14):
            first_row = wide[i, layer, PAD : PAD + 1, :]
            last_row = wide[i, layer, PAD + FACE - 1 : PAD + FACE, :]
            wide[i, layer, PAD - 2 : PAD - 1, :] = first_row
            wide[i, layer, PAD - 1 : PAD, :] = first_row
            wide[i, layer, PAD + FACE : PAD + FACE + 1, :] = last_row
            wide[i, layer, PAD + FACE + 1 : PAD + FACE + 2, :] = last_row

    pl.semaphore_wait(
        barrier, 21 + has_below.astype(jnp.int32) + has_above.astype(jnp.int32)
    )

    def exchange(kind, n, step):
        me, device = phases[n]
        return pltpu.make_async_remote_copy(
            src_ref=slots.at[kind, n, me],
            dst_ref=slots.at[kind, n, me],
            send_sem=rsend.at[kind, n, step],
            recv_sem=rrecv.at[kind, n, me],
            device_id=device((me + step) % 8),
            device_id_type=MESH,
        )

    def send(kind, n, value):
        slots[kind, n, pl.ds(phases[n][0], 1)] = value[None]
        for step in range(1, 8):
            exchange(kind, n, step).start()

    def receive(kind, n, op):
        me, device = phases[n]
        for step in range(1, 8):
            other = (me + step) % 8
            pltpu.make_async_remote_copy(
                src_ref=slots.at[kind, n, me],
                dst_ref=slots.at[kind, n, other],
                send_sem=rsend.at[kind, n, step],
                recv_sem=rrecv.at[kind, n, other],
                device_id=device(other),
                device_id_type=MESH,
            ).wait_recv()
        held = slots[kind, n, 0]
        for j in range(1, 8):
            held = op(held, slots[kind, n, j])
        for step in range(1, 8):
            exchange(kind, n, step).wait_send()
        return held

    send(0, 0, limit)

    sides = ((has_below, has_above, above_id), (has_above, has_below, below_id))

    def halo_copy(side, f):
        return pltpu.make_async_remote_copy(
            src_ref=state_hbm.at[f],
            dst_ref=halo[side][f].at[0],
            send_sem=hsend.at[side, f],
            recv_sem=hrecv.at[side, f],
            device_id=sides[side][2],
            device_id_type=MESH,
        )

    for fields in ORDER:
        for f in fields:
            for side in range(2):

                @pl.when(sides[side][1])
                def _():
                    halo_copy(side, f).start()

    lane = lax.broadcasted_iota(jnp.int32, (ROWS, FACE), 1)
    row = lax.broadcasted_iota(jnp.int32, (ROWS, FACE), 0)
    first, last, top = lane == 0, lane == FACE - 1, row == 0

    def after(x):
        return jnp.where(last, x, pltpu.roll(x, FACE - 1, 1))

    def before(x):
        return jnp.where(first, x, pltpu.roll(x, 1, 1))

    def local_flux(layer, fields, vorticity, low, high, carry=None):
        def load(i, k, offset):
            return wide[i, layer, pl.ds(k * ROWS + PAD + offset, ROWS), :]

        def cell(k, offset):
            v = [load(6 + i, k, offset) for i in range(8)]
            return {"u": v[:3], "p": v[3], "cs": v[4], "mu": v[5], "h": v[6], "nu": v[7]}

        def states(k, offset):
            return [load(f, k, offset) for f in range(6)]

        def body(k, carry):
            w0, q0 = states(k, 0), cell(k, 0)
            w1, q1 = states(k, 1), cell(k, 1)
            pm, p2 = load(9, k, -1), load(9, k, 2)
            s0 = sensor(pm, q0["p"], q1["p"])
            s1 = sensor(q0["p"], q1["p"], p2)
            g = face_flux(2, states(k, -1), w0, w1, states(k, 2), q0, q1, s0, s1, fields)
            turned = [pltpu.roll(x, 1, 0) for x in g]
            total = [x - jnp.where(top, c, y) for x, y, c in zip(g, turned, carry)]
            w1 = [after(x) for x in w0]
            w2 = [after(x) for x in w1]
            wm = [before(x) for x in w0]
            q1 = {n: after(q0[n]) for n in ("p", "cs", "mu", "h", "nu")}
            q1["u"] = [after(x) for x in q0["u"]]
            s0 = sensor(before(q0["p"]), q0["p"], q1["p"])
            g = face_flux(3, wm, w0, w1, w2, q0, q1, s0, after(s0), fields)
            edge = edge_flux(3, w0, w1, q0, s0, fields)
            total = [
                t + (x - jnp.where(first, e, pltpu.roll(x, 1, 1)))
                for t, x, e in zip(total, g, edge)
            ]
            at = rows_of(k)
            for f, x in zip(fields, total):
                part[f, layer, at, :] = x
            if vorticity:
                u1 = [load(6, k, 1), load(8, k, 1)]
                d2u0 = 0.5 * (u1[0] - load(6, k, -1))
                d2u2 = 0.5 * (u1[1] - load(8, k, -1))
                d3u0 = 0.5 * (q1["u"][0] - before(q0["u"][0]))
                d3u1 = 0.5 * (q1["u"][1] - before(q0["u"][1]))
                vort[0, layer, at, :] = d2u2 - d3u1
                vort[1, layer, at, :] = d3u0
                vort[2, layer, at, :] = d2u0
            return tuple(turned)

        if carry is None:
            w0, q0 = states(0, 0), cell(0, 0)
            s0 = sensor(load(9, 0, -1), q0["p"], load(9, 0, 1))
            carry = edge_flux(2, w0, states(0, 1), q0, s0, fields)
        return lax.fori_loop(low, high, body, tuple(carry))

    for layer in range(2):
        local_flux(layer, (0,), False, 0, STEPS)
    send(0, 1, receive(0, 0, jnp.minimum))

    def one_if(condition):
        return jnp.where(condition, 1, 0)

    loads[2].wait()
    up = jnp.minimum(blk + 1, chain - 1)
    t, r2, r3 = [flags[i, comp, blk] * one_if(has_below) for i in range(3)]
    lower = (t, t * r3 + (1 - t) * r2, t * r2 + (1 - t) * r3)
    upper = tuple(flags[i, comp, up] * one_if(has_above) for i in range(3))

    turns = []
    for t, flip_rows, flip_lanes in (lower, upper):
        masks = [jnp.broadcast_to(x, (ROWS, FACE)) > 0 for x in (t, flip_rows, flip_lanes)]
        signs = [1.0 - 2.0 * x.astype(jnp.float32) for x in (flip_rows, flip_lanes)]
        turns.append((masks, signs))

    def arrive(fields):
        for side in range(2):
            for f in fields:

                @pl.when(sides[side][0])
                def _():
                    halo_copy(side, f).wait_recv()

                @pl.when(jnp.logical_not(sides[side][0]))
                def _():
                    for layer in range(2):
                        halo[side][f][0, layer] = state[f, side]

        for side in range(2):
            for f in fields:
                for layer in range(2):
                    source = halo[side][{2: 3, 3: 2}.get(f, f)]
                    halo[side][f][1, layer] = source[0, layer].T

        def place(k, _):
            pair = (rows_of(k), rows_of(STEPS - 1 - k))
            for side in range(2):
                (turn, reverse_rows, reverse_lanes), signs = turns[side]
                for f in fields:
                    buf = halo[side][f]
                    for layer in range(2):
                        x = [
                            jnp.where(turn, buf[1, layer, at, :], buf[0, layer, at, :])
                            for at in pair
                        ]
                        flipped = [jnp.take_along_axis(y, ROWS - 1 - row, axis=0) for y in x]
                        for i in range(2):
                            y = jnp.where(reverse_rows, flipped[1 - i], x[i])
                            z = jnp.take_along_axis(y, FACE - 1 - lane, axis=1)
                            y = jnp.where(reverse_lanes, z, y)
                            if f in (2, 3):
                                y = y * signs[f - 2]
                            ghost[side, f, layer, pair[i], :] = y
            return 0

        lax.fori_loop(0, STEPS // 2, place, 0)

    arrive(ORDER[0])
    arrive(ORDER[1])
    send(0, 2, receive(0, 1, jnp.minimum))
    for fields in ORDER[2:]:
        arrive(fields)

    def own(i, layer, k):
        return wide[i, layer, pl.ds(pl.multiple_of(k * ROWS + PAD, ROWS), ROWS), :]

    def density_rows(k, total):
        at = rows_of(k)
        rho, p, un, cs = [], [], [], []
        for side, layer in ((0, 0), (0, 1), (None, 0), (None, 1), (1, 0), (1, 1)):
            if side is None:
                rho.append(own(0, layer, k))
                un.append(own(6, layer, k))
                p.append(own(9, layer, k))
                cs.append(own(10, layer, k))
            else:
                w = [ghost[side, f, layer, at, :] for f in range(5)]
                q = primitives(w + [w[0]])
                rho.append(w[0])
                un.append(q["u"][0])
                p.append(q["p"])
                cs.append(q["cs"])
        s = [None] + [sensor(p[i - 1], p[i], p[i + 1]) for i in range(1, 5)]
        g = []
        for i in range(1, 4):
            half = 0.5 * ((jnp.abs(un[i]) + cs[i]) + (jnp.abs(un[i + 1]) + cs[i + 1]))
            e2 = 0.25 * jnp.maximum(s[i], s[i + 1])
            b = half * jnp.maximum(0.0, 0.03125 - e2)
            c = half * e2 + 3.0 * b
            g.append(
                0.5 * (rho[i] * un[i] + rho[i + 1] * un[i + 1])
                - c * (rho[i + 1] - rho[i])
                + b * (rho[i + 2] - rho[i - 1])
            )
        for layer in range(2):
            z = (part[0, layer, at, :] + (g[layer + 1] - g[layer])) / volume[layer, at, :]
            change[0, layer, at, :] = z
            total = total + z * z
        return total

    def density(k, total):
        return density_rows(2 * k + 1, density_rows(2 * k, total))

    total = lax.fori_loop(0, STEPS // 2, density, jnp.zeros((ROWS, FACE), jnp.float32))
    send(1, 0, total)

    def rest(k, _):
        at = rows_of(k)
        w, q = [], []
        for side, layer in ((0, 0), (0, 1), (None, 0), (None, 1), (1, 0), (1, 1)):
            if side is None:
                w.append([own(f, layer, k) for f in range(6)])
                v = [own(6 + i, layer, k) for i in range(8)]
                q.append({"u": v[:3], "p": v[3], "cs": v[4], "mu": v[5], "h": v[6], "nu": v[7]})
            else:
                w.append([ghost[side, f, layer, at, :] for f in range(6)])
                q.append(primitives(w[-1]))
        s = [None] + [sensor(q[i - 1]["p"], q[i]["p"], q[i + 1]["p"]) for i in range(1, 5)]
        fields = range(1, 6)
        g = [
            face_flux(1, w[i - 1], w[i], w[i + 1], w[i + 2], q[i], q[i + 1], s[i], s[i + 1], fields)
            for i in range(1, 4)
        ]
        for layer in range(2):
            i = layer + 2
            vol = volume[layer, at, :]
            inv = 1.0 / vol
            d1u1 = 0.5 * (q[i + 1]["u"][1] - q[i - 1]["u"][1])
            d1u2 = 0.5 * (q[i + 1]["u"][2] - q[i - 1]["u"][2])
            w1 = vort[0, layer, at, :]
            w2 = vort[1, layer, at, :] - d1u2
            w3 = d1u1 - vort[2, layer, at, :]
            spin = jnp.sqrt(w1 * w1 + w2 * w2 + w3 * w3 + 1e-6)
            ratio = q[i]["nu"] / distance[layer, at, :]
            source = 0.1355 * spin * w[i][5] - 3.239 * w[i][0] * (ratio * ratio)
            for f in fields:
                r = part[f, layer, at, :] + (g[layer + 1][f - 1] - g[layer][f - 1])
                if f == 5:
                    r = r - vol * source
                change[f, layer, at, :] = base[f, layer, at, :] - least * (r * inv)
            change[0, layer, at, :] = base[0, layer, at, :] - least * change[0, layer, at, :]
        return 0

    others = (1, 2, 3, 4, 5)
    held = local_flux(0, others, True, 0, 8)
    least = receive(0, 2, jnp.minimum)
    least = jnp.broadcast_to(jnp.min(least, axis=(0, 1), keepdims=True), (ROWS, FACE))
    send(1, 1, receive(1, 0, jnp.add))
    local_flux(0, others, True, 8, STEPS, held)
    local_flux(1, others, True, 0, STEPS)
    send(1, 2, receive(1, 1, jnp.add))
    loads[3].wait()
    loads[4].wait()
    lax.fori_loop(0, STEPS, rest, 0)
    store = pltpu.make_async_copy(change, new_hbm, load_sem.at[5])
    store.start()
    for side in range(2):
        for f in range(6):

            @pl.when(sides[side][1])
            def _():
                halo_copy(side, f).wait_send()

    total_out[...] = jnp.sum(receive(1, 2, jnp.add), axis=(0, 1), keepdims=True)
    store.wait()


def entry(*args):
    names = ("flags", "state", "base", "volume", "distance", "wide", "part", "vort")
    names = names + ("change", "ghost", "slots")
    refs = {"inputs": args[:5], "outputs": args[5:7]}
    refs.update(zip(names, args[7:18]))
    refs["halo"] = args[18:30]
    refs["sems"] = args[30:]
    kernel(refs)


def per_device(base_state, section_state, volume, distance, orientation):
    f32 = functools.partial(jax.ShapeDtypeStruct, dtype=jnp.float32)
    scratch = functools.partial(VMEM, dtype=jnp.float32)
    hbm = pl.BlockSpec(memory_space=pl.ANY)
    plane = (2, FACE, FACE)
    dma = pltpu.SemaphoreType.DMA
    flags = jnp.transpose(orientation, (2, 0, 1))
    new, total = pl.pallas_call(
        entry,
        out_shape=(f32((6,) + plane), f32((1, 1))),
        in_specs=[hbm] * 5,
        out_specs=(hbm, pl.BlockSpec(memory_space=VMEM)),
        scratch_shapes=[
            pltpu.SMEM(flags.shape, jnp.int32),
            scratch((6,) + plane),
            scratch((6,) + plane),
            scratch(plane),
            scratch(plane),
            scratch((14, 2, FACE + 2 * PAD, FACE)),
            scratch((6,) + plane),
            scratch((3,) + plane),
            scratch((6,) + plane),
            scratch((2, 6) + plane),
            scratch((2, 3, 8, 8, FACE)),
        ]
        + [scratch((2,) + plane)] * 12
        + [dma((6,)), dma((2, 6)), dma((2, 6)), dma((2, 3, 8)), dma((2, 3, 8))],
        compiler_params=pltpu.CompilerParams(collective_id=1, has_side_effects=True),
        cost_estimate=pl.CostEstimate(
            flops=80_000_000, bytes_accessed=4_000_000, transcendentals=800_000
        ),
        name="section",
    )(flags, section_state[0, 0], volume[0, 0], distance[0, 0], base_state[0, 0])
    cells = lax.axis_size("comp") * lax.axis_size("blk") * 2 * FACE * FACE
    return new[None, None], jnp.sqrt(total[0, 0] / cells)


def solution(mesh):
    wide = P("comp", "blk", None, None, None, None)
    cell = P("comp", "blk", None, None, None)
    return jax.shard_map(
        per_device,
        mesh=mesh,
        in_specs=(wide, wide, cell, cell, P()),
        out_specs=(wide, P()),
        check_vma=False,
    )
```

```python
import functools

import jax
import jax.numpy as jnp
from jax import lax
from jax.experimental import pallas as pl
from jax.experimental.pallas import tpu as pltpu
from jax.sharding import PartitionSpec as P

GAMMA = 1.4
HEAT = 1.4 / (0.4 * 0.72)
CUBE = 7.1 * 7.1 * 7.1
MESH = pl.DeviceIdType.MESH
VMEM = pltpu.VMEM
FACE = 128
PAD = 8


def primitives(w):
    inv = 1.0 / w[0]
    u = [w[1] * inv, w[2] * inv, w[3] * inv]
    kinetic = 0.5 * (w[1] * u[0] + w[2] * u[1] + w[3] * u[2])
    p = 0.4 * (w[4] - kinetic)
    heat = p * inv
    cs = jnp.sqrt(GAMMA * heat)
    chi = w[5] * 20.0
    cubed = chi * chi * chi
    mu = w[5] * cubed / (cubed + CUBE)
    h = 0.5 * (u[0] * u[0] + u[1] * u[1] + u[2] * u[2]) + HEAT * heat
    return {"u": u, "p": p, "cs": cs, "mu": mu, "h": h, "nu": w[5] * inv}


def sensor(before, middle, after):
    twice = 2.0 * middle
    total = after + before
    return jnp.abs(total - twice) / (total + twice)


def face_flux(a, wm, w0, w1, w2, q0, q1, s0, s1, fields=range(6)):
    un0, un1 = q0["u"][a - 1], q1["u"][a - 1]
    half = 0.5 * ((jnp.abs(un0) + q0["cs"]) + (jnp.abs(un1) + q1["cs"]))
    e2 = 0.25 * jnp.maximum(s0, s1)
    e4 = jnp.maximum(0.0, 0.03125 - e2)
    b = half * e4
    c = half * e2 + 3.0 * b
    h0, h1 = 0.5 * un0, 0.5 * un1
    muf = 0.05 + 0.5 * (q0["mu"] + q1["mu"])
    out = []
    for f in fields:
        c0, c1 = w0[f], w1[f]
        if f == 4:
            c0, c1 = c0 + q0["p"], c1 + q1["p"]
        g = c0 * h0 + c1 * h1
        if f == a:
            g = g + 0.5 * (q0["p"] + q1["p"])
        g = g - c * (w1[f] - w0[f]) + b * (w2[f] - wm[f])
        if 1 <= f <= 3:
            g = g - muf * (q1["u"][f - 1] - q0["u"][f - 1])
        elif f == 4:
            g = g - muf * (q1["h"] - q0["h"])
        elif f == 5:
            g = g - (0.075 + 0.75 * (w0[5] + w1[5])) * (q1["nu"] - q0["nu"])
        out.append(g)
    return out


def edge_flux(a, w0, w1, q0, s0, fields=range(6)):
    un = q0["u"][a - 1]
    b = (jnp.abs(un) + q0["cs"]) * jnp.maximum(0.0, 0.03125 - 0.25 * s0)
    out = []
    for f in fields:
        c0 = w0[f] + q0["p"] if f == 4 else w0[f]
        g = c0 * un
        if f == a:
            g = g + q0["p"]
        out.append(g + b * (w1[f] - w0[f]))
    return out


ROWS = 8
STEPS = FACE // ROWS
ORDER = ((2, 3), (0,), (1,), (4,), (5,))


def kernel(refs):
    comp, blk = lax.axis_index("comp"), lax.axis_index("blk")
    chain = lax.axis_size("blk")
    flags_hbm, state_hbm, volume_hbm, distance_hbm, base_hbm = refs["inputs"]
    change, total_out = refs["outputs"]
    flags, base = refs["flags"], refs["base"]
    state, volume, distance = refs["state"], refs["volume"], refs["distance"]
    wide, part, vort = refs["wide"], refs["part"], refs["vort"]
    ghost, slots = refs["ghost"], refs["slots"]
    halo = (refs["halo"][:6], refs["halo"][6:])
    load_sem, hsend, hrecv, rsend, rrecv = refs["sems"]

    low, high = blk % 8, blk // 8
    phases = (
        (low, lambda j: (comp, high * 8 + j)),
        (comp, lambda j: (j, blk)),
        (high, lambda j: (comp, j * 8 + low)),
    )
    has_below, has_above = blk > 0, blk < chain - 1
    below_id = (comp, jnp.maximum(blk - 1, 0))
    above_id = (comp, jnp.minimum(blk + 1, chain - 1))

    loads = [
        pltpu.make_async_copy(source, target, load_sem.at[i])
        for i, (source, target) in enumerate(
            (
                (state_hbm, state),
                (volume_hbm, volume),
                (flags_hbm, flags),
                (distance_hbm, distance),
                (base_hbm, base),
            )
        )
    ]
    for copy in loads:
        copy.start()

    barrier = pltpu.get_barrier_semaphore()
    for has, device in ((has_below, below_id), (has_above, above_id)):

        @pl.when(has)
        def _():
            pl.semaphore_signal(barrier, inc=1, device_id=device, device_id_type=MESH)

    for me, device in phases:
        for step in range(1, 8):
            pl.semaphore_signal(
                barrier, inc=1, device_id=device((me + step) % 8), device_id_type=MESH
            )

    def rows_of(k):
        return pl.ds(pl.multiple_of(k * ROWS, ROWS), ROWS)

    pl.semaphore_wait(
        barrier, 21 + has_below.astype(jnp.int32) + has_above.astype(jnp.int32)
    )

    def exchange(kind, n, step):
        me, device = phases[n]
        return pltpu.make_async_remote_copy(
            src_ref=slots.at[kind, n, me],
            dst_ref=slots.at[kind, n, me],
            send_sem=rsend.at[kind, n, step],
            recv_sem=rrecv.at[kind, n, me],
            device_id=device((me + step) % 8),
            device_id_type=MESH,
        )

    def send(kind, n, value):
        slots[kind, n, pl.ds(phases[n][0], 1)] = value[None]
        for step in range(1, 8):
            exchange(kind, n, step).start()

    def receive(kind, n, op):
        me, device = phases[n]
        for step in range(1, 8):
            other = (me + step) % 8
            pltpu.make_async_remote_copy(
                src_ref=slots.at[kind, n, me],
                dst_ref=slots.at[kind, n, other],
                send_sem=rsend.at[kind, n, step],
                recv_sem=rrecv.at[kind, n, other],
                device_id=device(other),
                device_id_type=MESH,
            ).wait_recv()
        held = slots[kind, n, 0]
        for j in range(1, 8):
            held = op(held, slots[kind, n, j])
        for step in range(1, 8):
            exchange(kind, n, step).wait_send()
        return held

    sides = ((has_below, has_above, above_id), (has_above, has_below, below_id))

    def halo_copy(side, f):
        return pltpu.make_async_remote_copy(
            src_ref=state_hbm.at[f],
            dst_ref=halo[side][f].at[0],
            send_sem=hsend.at[side, f],
            recv_sem=hrecv.at[side, f],
            device_id=sides[side][2],
            device_id_type=MESH,
        )

    def send_halo(fields):
        for f in fields:
            for side in range(2):

                @pl.when(sides[side][1])
                def _():
                    halo_copy(side, f).start()

    send_halo(ORDER[0])
    loads[0].wait()
    loads[1].wait()

    def fill_rows(k, least):
        at = rows_of(k)
        to = pl.ds(pl.multiple_of(k * ROWS + PAD, ROWS), ROWS)
        for layer in range(2):
            w = [state[f, layer, at, :] for f in range(6)]
            q = primitives(w)
            u = q["u"]
            for f in range(6):
                wide[f, layer, to, :] = w[f]
            for i, x in enumerate(u + [q["p"], q["cs"], q["mu"], q["h"], q["nu"]]):
                wide[6 + i, layer, to, :] = x
            speed = (jnp.abs(u[0]) + q["cs"]) + (jnp.abs(u[1]) + q["cs"]) + (jnp.abs(u[2]) + q["cs"])
            least = jnp.minimum(least, volume[layer, at, :] / speed)
        return least

    def fill(k, least):
        return fill_rows(2 * k + 1, fill_rows(2 * k, least))

    limit = lax.fori_loop(0, STEPS // 2, fill, jnp.full((ROWS, FACE), jnp.inf, jnp.float32))
    for layer in range(2):
        for i in range(14):
            first_row = wide[i, layer, PAD : PAD + 1, :]
            last_row = wide[i, layer, PAD + FACE - 1 : PAD + FACE, :]
            wide[i, layer, PAD - 2 : PAD - 1, :] = first_row
            wide[i, layer, PAD - 1 : PAD, :] = first_row
            wide[i, layer, PAD + FACE : PAD + FACE + 1, :] = last_row
            wide[i, layer, PAD + FACE + 1 : PAD + FACE + 2, :] = last_row

    send(0, 0, limit)
    for fields in ORDER[1:]:
        send_halo(fields)

    lane = lax.broadcasted_iota(jnp.int32, (ROWS, FACE), 1)
    row = lax.broadcasted_iota(jnp.int32, (ROWS, FACE), 0)
    first, last, top = lane == 0, lane == FACE - 1, row == 0

    def after(x):
        return jnp.where(last, x, pltpu.roll(x, FACE - 1, 1))

    def before(x):
        return jnp.where(first, x, pltpu.roll(x, 1, 1))

    def local_flux(layer, fields, vorticity, low, high, carry=None):
        def load(i, k, offset):
            return wide[i, layer, pl.ds(k * ROWS + PAD + offset, ROWS), :]

        def cell(k, offset):
            v = [load(6 + i, k, offset) for i in range(8)]
            return {"u": v[:3], "p": v[3], "cs": v[4], "mu": v[5], "h": v[6], "nu": v[7]}

        def states(k, offset):
            return [load(f, k, offset) for f in range(6)]

        def body(k, carry):
            w0, q0 = states(k, 0), cell(k, 0)
            w1, q1 = states(k, 1), cell(k, 1)
            pm, p2 = load(9, k, -1), load(9, k, 2)
            s0 = sensor(pm, q0["p"], q1["p"])
            s1 = sensor(q0["p"], q1["p"], p2)
            g = face_flux(2, states(k, -1), w0, w1, states(k, 2), q0, q1, s0, s1, fields)
            turned = [pltpu.roll(x, 1, 0) for x in g]
            total = [x - jnp.where(top, c, y) for x, y, c in zip(g, turned, carry)]
            w1 = [after(x) for x in w0]
            w2 = [after(x) for x in w1]
            wm = [before(x) for x in w0]
            q1 = {n: after(q0[n]) for n in ("p", "cs", "mu", "h", "nu")}
            q1["u"] = [after(x) for x in q0["u"]]
            s0 = sensor(before(q0["p"]), q0["p"], q1["p"])
            g = face_flux(3, wm, w0, w1, w2, q0, q1, s0, after(s0), fields)
            edge = edge_flux(3, w0, w1, q0, s0, fields)
            total = [
                t + (x - jnp.where(first, e, pltpu.roll(x, 1, 1)))
                for t, x, e in zip(total, g, edge)
            ]
            at = rows_of(k)
            for f, x in zip(fields, total):
                part[f, layer, at, :] = x
            if vorticity:
                u1 = [load(6, k, 1), load(8, k, 1)]
                d2u0 = 0.5 * (u1[0] - load(6, k, -1))
                d2u2 = 0.5 * (u1[1] - load(8, k, -1))
                d3u0 = 0.5 * (q1["u"][0] - before(q0["u"][0]))
                d3u1 = 0.5 * (q1["u"][1] - before(q0["u"][1]))
                vort[0, layer, at, :] = d2u2 - d3u1
                vort[1, layer, at, :] = d3u0
                vort[2, layer, at, :] = d2u0
            return tuple(turned)

        if carry is None:
            w0, q0 = states(0, 0), cell(0, 0)
            s0 = sensor(load(9, 0, -1), q0["p"], load(9, 0, 1))
            carry = edge_flux(2, w0, states(0, 1), q0, s0, fields)
        return lax.fori_loop(low, high, body, tuple(carry))

    for layer in range(2):
        local_flux(layer, (0,), False, 0, STEPS)

    def one_if(condition):
        return jnp.where(condition, 1, 0)

    loads[2].wait()
    up = jnp.minimum(blk + 1, chain - 1)
    t, r2, r3 = [flags[i, comp, blk] * one_if(has_below) for i in range(3)]
    lower = (t, t * r3 + (1 - t) * r2, t * r2 + (1 - t) * r3)
    upper = tuple(flags[i, comp, up] * one_if(has_above) for i in range(3))

    turns = []
    for t, flip_rows, flip_lanes in (lower, upper):
        masks = [jnp.broadcast_to(x, (ROWS, FACE)) > 0 for x in (t, flip_rows, flip_lanes)]
        signs = [1.0 - 2.0 * x.astype(jnp.float32) for x in (flip_rows, flip_lanes)]
        turns.append((masks, signs))

    def arrive(fields):
        for side in range(2):
            for f in fields:

                @pl.when(sides[side][0])
                def _():
                    halo_copy(side, f).wait_recv()

                @pl.when(jnp.logical_not(sides[side][0]))
                def _():
                    for layer in range(2):
                        halo[side][f][0, layer] = state[f, side]

        for side in range(2):
            for f in fields:
                for layer in range(2):
                    source = halo[side][{2: 3, 3: 2}.get(f, f)]
                    halo[side][f][1, layer] = source[0, layer].T

        def place(k, _):
            pair = (rows_of(k), rows_of(STEPS - 1 - k))
            for side in range(2):
                (turn, reverse_rows, reverse_lanes), signs = turns[side]
                for f in fields:
                    buf = halo[side][f]
                    for layer in range(2):
                        x = [
                            jnp.where(turn, buf[1, layer, at, :], buf[0, layer, at, :])
                            for at in pair
                        ]
                        flipped = [jnp.take_along_axis(y, ROWS - 1 - row, axis=0) for y in x]
                        for i in range(2):
                            y = jnp.where(reverse_rows, flipped[1 - i], x[i])
                            z = jnp.take_along_axis(y, FACE - 1 - lane, axis=1)
                            y = jnp.where(reverse_lanes, z, y)
                            if f in (2, 3):
                                y = y * signs[f - 2]
                            ghost[side, f, layer, pair[i], :] = y
            return 0

        lax.fori_loop(0, STEPS // 2, place, 0)

    arrive(ORDER[0])
    arrive(ORDER[1])
    send(0, 1, receive(0, 0, jnp.minimum))
    arrive(ORDER[2])
    arrive(ORDER[3])

    def own(i, layer, k):
        return wide[i, layer, pl.ds(pl.multiple_of(k * ROWS + PAD, ROWS), ROWS), :]

    def density_rows(k, total):
        at = rows_of(k)
        rho, p, un, cs = [], [], [], []
        for side, layer in ((0, 0), (0, 1), (None, 0), (None, 1), (1, 0), (1, 1)):
            if side is None:
                rho.append(own(0, layer, k))
                un.append(own(6, layer, k))
                p.append(own(9, layer, k))
                cs.append(own(10, layer, k))
            else:
                w = [ghost[side, f, layer, at, :] for f in range(5)]
                q = primitives(w + [w[0]])
                rho.append(w[0])
                un.append(q["u"][0])
                p.append(q["p"])
                cs.append(q["cs"])
        s = [None] + [sensor(p[i - 1], p[i], p[i + 1]) for i in range(1, 5)]
        g = []
        for i in range(1, 4):
            half = 0.5 * ((jnp.abs(un[i]) + cs[i]) + (jnp.abs(un[i + 1]) + cs[i + 1]))
            e2 = 0.25 * jnp.maximum(s[i], s[i + 1])
            b = half * jnp.maximum(0.0, 0.03125 - e2)
            c = half * e2 + 3.0 * b
            g.append(
                0.5 * (rho[i] * un[i] + rho[i + 1] * un[i + 1])
                - c * (rho[i + 1] - rho[i])
                + b * (rho[i + 2] - rho[i - 1])
            )
        for layer in range(2):
            z = (part[0, layer, at, :] + (g[layer + 1] - g[layer])) / volume[layer, at, :]
            change[0, layer, at, :] = z
            total = total + z * z
        return total

    def density(k, total):
        return density_rows(2 * k + 1, density_rows(2 * k, total))

    total = lax.fori_loop(0, STEPS // 2, density, jnp.zeros((ROWS, FACE), jnp.float32))
    send(1, 0, total)
    send(0, 2, receive(0, 1, jnp.minimum))
    arrive(ORDER[4])

    def rest(k, _):
        at = rows_of(k)
        w, q = [], []
        for side, layer in ((0, 0), (0, 1), (None, 0), (None, 1), (1, 0), (1, 1)):
            if side is None:
                w.append([own(f, layer, k) for f in range(6)])
                v = [own(6 + i, layer, k) for i in range(8)]
                q.append({"u": v[:3], "p": v[3], "cs": v[4], "mu": v[5], "h": v[6], "nu": v[7]})
            else:
                w.append([ghost[side, f, layer, at, :] for f in range(6)])
                q.append(primitives(w[-1]))
        s = [None] + [sensor(q[i - 1]["p"], q[i]["p"], q[i + 1]["p"]) for i in range(1, 5)]
        fields = range(1, 6)
        g = [
            face_flux(1, w[i - 1], w[i], w[i + 1], w[i + 2], q[i], q[i + 1], s[i], s[i + 1], fields)
            for i in range(1, 4)
        ]
        for layer in range(2):
            i = layer + 2
            vol = volume[layer, at, :]
            inv = 1.0 / vol
            d1u1 = 0.5 * (q[i + 1]["u"][1] - q[i - 1]["u"][1])
            d1u2 = 0.5 * (q[i + 1]["u"][2] - q[i - 1]["u"][2])
            w1 = vort[0, layer, at, :]
            w2 = vort[1, layer, at, :] - d1u2
            w3 = d1u1 - vort[2, layer, at, :]
            spin = jnp.sqrt(w1 * w1 + w2 * w2 + w3 * w3 + 1e-6)
            ratio = q[i]["nu"] / distance[layer, at, :]
            source = 0.1355 * spin * w[i][5] - 3.239 * w[i][0] * (ratio * ratio)
            for f in fields:
                r = part[f, layer, at, :] + (g[layer + 1][f - 1] - g[layer][f - 1])
                if f == 5:
                    r = r - vol * source
                change[f, layer, at, :] = base[f, layer, at, :] - least * (r * inv)
            change[0, layer, at, :] = base[0, layer, at, :] - least * change[0, layer, at, :]
        return 0

    others = (1, 2, 3, 4, 5)
    held = local_flux(0, others, True, 0, 4)
    send(1, 1, receive(1, 0, jnp.add))
    local_flux(0, others, True, 4, STEPS, held)
    local_flux(1, others, True, 0, STEPS)
    send(1, 2, receive(1, 1, jnp.add))
    least = receive(0, 2, jnp.minimum)
    least = jnp.broadcast_to(jnp.min(least, axis=(0, 1), keepdims=True), (ROWS, FACE))
    loads[3].wait()
    loads[4].wait()
    lax.fori_loop(0, STEPS, rest, 0)
    for side in range(2):
        for f in range(6):

            @pl.when(sides[side][1])
            def _():
                halo_copy(side, f).wait_send()

    cells = lax.axis_size("comp") * chain * 2 * FACE * FACE
    norm = jnp.sum(receive(1, 2, jnp.add), axis=(0, 1), keepdims=True)
    total_out[...] = jnp.sqrt(norm / cells)


def entry(*args):
    names = ("flags", "state", "base", "volume", "distance", "wide", "part", "vort")
    names = names + ("ghost", "slots")
    refs = {"inputs": args[:5], "outputs": args[5:7]}
    refs.update(zip(names, args[7:17]))
    refs["halo"] = args[17:29]
    refs["sems"] = args[29:]
    kernel(refs)


def per_device(base_state, section_state, volume, distance, orientation):
    f32 = functools.partial(jax.ShapeDtypeStruct, dtype=jnp.float32)
    scratch = functools.partial(VMEM, dtype=jnp.float32)
    hbm = pl.BlockSpec(memory_space=pl.ANY)
    plane = (2, FACE, FACE)
    dma = pltpu.SemaphoreType.DMA
    flags = jnp.transpose(orientation, (2, 0, 1))
    new, total = pl.pallas_call(
        entry,
        out_shape=(scratch((6,) + plane), f32((1, 1))),
        in_specs=[hbm] * 5,
        out_specs=(pl.BlockSpec(memory_space=VMEM),) * 2,
        scratch_shapes=[
            pltpu.SMEM(flags.shape, jnp.int32),
            scratch((6,) + plane),
            scratch((6,) + plane),
            scratch(plane),
            scratch(plane),
            scratch((14, 2, FACE + 2 * PAD, FACE)),
            scratch((6,) + plane),
            scratch((3,) + plane),
            scratch((2, 6) + plane),
            scratch((2, 3, 8, 8, FACE)),
        ]
        + [scratch((2,) + plane)] * 12
        + [dma((5,)), dma((2, 6)), dma((2, 6)), dma((2, 3, 8)), dma((2, 3, 8))],
        compiler_params=pltpu.CompilerParams(collective_id=1, has_side_effects=True),
        cost_estimate=pl.CostEstimate(
            flops=80_000_000, bytes_accessed=4_000_000, transcendentals=800_000
        ),
        name="section",
    )(flags, section_state[0, 0], volume[0, 0], distance[0, 0], base_state[0, 0])
    return new[None, None], total[0, 0]


def solution(mesh):
    wide = P("comp", "blk", None, None, None, None)
    cell = P("comp", "blk", None, None, None)
    return jax.shard_map(
        per_device,
        mesh=mesh,
        in_specs=(wide, wide, cell, cell, P()),
        out_specs=(wide, P()),
        check_vma=False,
    )
```

```python
import functools

import jax
import jax.numpy as jnp
from jax import lax
from jax.experimental import pallas as pl
from jax.experimental.pallas import tpu as pltpu
from jax.sharding import PartitionSpec as P

GAMMA = 1.4
HEAT = 1.4 / (0.4 * 0.72)
CUBE = 7.1 * 7.1 * 7.1
MESH = pl.DeviceIdType.MESH
VMEM = pltpu.VMEM
FACE = 128
PAD = 8


def primitives(w):
    inv = 1.0 / w[0]
    u = [w[1] * inv, w[2] * inv, w[3] * inv]
    kinetic = 0.5 * (w[1] * u[0] + w[2] * u[1] + w[3] * u[2])
    p = 0.4 * (w[4] - kinetic)
    heat = p * inv
    cs = jnp.sqrt(GAMMA * heat)
    chi = w[5] * 20.0
    cubed = chi * chi * chi
    mu = w[5] * cubed / (cubed + CUBE)
    h = 0.5 * (u[0] * u[0] + u[1] * u[1] + u[2] * u[2]) + HEAT * heat
    return {"u": u, "p": p, "cs": cs, "mu": mu, "h": h, "nu": w[5] * inv}


def sensor(before, middle, after):
    twice = 2.0 * middle
    total = after + before
    return jnp.abs(total - twice) / (total + twice)


def face_flux(a, wm, w0, w1, w2, q0, q1, s0, s1, fields=range(6)):
    un0, un1 = q0["u"][a - 1], q1["u"][a - 1]
    half = 0.5 * ((jnp.abs(un0) + q0["cs"]) + (jnp.abs(un1) + q1["cs"]))
    e2 = 0.25 * jnp.maximum(s0, s1)
    e4 = jnp.maximum(0.0, 0.03125 - e2)
    b = half * e4
    c = half * e2 + 3.0 * b
    h0, h1 = 0.5 * un0, 0.5 * un1
    muf = 0.05 + 0.5 * (q0["mu"] + q1["mu"])
    out = []
    for f in fields:
        c0, c1 = w0[f], w1[f]
        if f == 4:
            c0, c1 = c0 + q0["p"], c1 + q1["p"]
        g = c0 * h0 + c1 * h1
        if f == a:
            g = g + 0.5 * (q0["p"] + q1["p"])
        g = g - c * (w1[f] - w0[f]) + b * (w2[f] - wm[f])
        if 1 <= f <= 3:
            g = g - muf * (q1["u"][f - 1] - q0["u"][f - 1])
        elif f == 4:
            g = g - muf * (q1["h"] - q0["h"])
        elif f == 5:
            g = g - (0.075 + 0.75 * (w0[5] + w1[5])) * (q1["nu"] - q0["nu"])
        out.append(g)
    return out


def edge_flux(a, w0, w1, q0, s0, fields=range(6)):
    un = q0["u"][a - 1]
    b = (jnp.abs(un) + q0["cs"]) * jnp.maximum(0.0, 0.03125 - 0.25 * s0)
    out = []
    for f in fields:
        c0 = w0[f] + q0["p"] if f == 4 else w0[f]
        g = c0 * un
        if f == a:
            g = g + q0["p"]
        out.append(g + b * (w1[f] - w0[f]))
    return out


ROWS = 8
STEPS = FACE // ROWS
ORDER = ((2, 3), (0,), (1,), (4,), (5,))


def kernel(refs):
    comp, blk = lax.axis_index("comp"), lax.axis_index("blk")
    chain = lax.axis_size("blk")
    flags_hbm, state_hbm, volume_hbm, distance_hbm, base_hbm = refs["inputs"]
    change, total_out = refs["outputs"]
    flags, base = refs["flags"], refs["base"]
    state, volume, distance = refs["state"], refs["volume"], refs["distance"]
    wide, part, vort = refs["wide"], refs["part"], refs["vort"]
    ghost, slots = refs["ghost"], refs["slots"]
    halo = (refs["halo"][:6], refs["halo"][6:])
    load_sem, hsend, hrecv, rsend, rrecv = refs["sems"]

    low, high = blk % 8, blk // 8
    phases = (
        (low, lambda j: (comp, high * 8 + j)),
        (comp, lambda j: (j, blk)),
        (high, lambda j: (comp, j * 8 + low)),
    )
    has_below, has_above = blk > 0, blk < chain - 1
    below_id = (comp, jnp.maximum(blk - 1, 0))
    above_id = (comp, jnp.minimum(blk + 1, chain - 1))

    loads = [
        pltpu.make_async_copy(source, target, load_sem.at[i])
        for i, (source, target) in enumerate(
            (
                (state_hbm, state),
                (volume_hbm, volume),
                (flags_hbm, flags),
                (distance_hbm, distance),
                (base_hbm, base),
            )
        )
    ]
    for copy in loads:
        copy.start()

    barrier = pltpu.get_barrier_semaphore()
    for has, device in ((has_below, below_id), (has_above, above_id)):

        @pl.when(has)
        def _():
            pl.semaphore_signal(barrier, inc=1, device_id=device, device_id_type=MESH)

    for me, device in phases:
        for step in range(1, 8):
            pl.semaphore_signal(
                barrier, inc=1, device_id=device((me + step) % 8), device_id_type=MESH
            )

    def rows_of(k):
        return pl.ds(pl.multiple_of(k * ROWS, ROWS), ROWS)

    pl.semaphore_wait(
        barrier, 21 + has_below.astype(jnp.int32) + has_above.astype(jnp.int32)
    )

    def exchange(kind, n, step):
        me, device = phases[n]
        return pltpu.make_async_remote_copy(
            src_ref=slots.at[kind, n, me],
            dst_ref=slots.at[kind, n, me],
            send_sem=rsend.at[kind, n],
            recv_sem=rrecv.at[kind, n],
            device_id=device((me + step) % 8),
            device_id_type=MESH,
        )

    def send(kind, n, value):
        slots[kind, n, pl.ds(phases[n][0], 1)] = value[None]
        for step in range(1, 8):
            exchange(kind, n, step).start()

    def receive(kind, n, op):
        seven = slots.at[kind, n, pl.ds(0, 7)]
        pltpu.make_async_copy(seven, seven, rrecv.at[kind, n]).wait()
        held = slots[kind, n, 0]
        for j in range(1, 8):
            held = op(held, slots[kind, n, j])
        return held

    sides = ((has_below, has_above, above_id), (has_above, has_below, below_id))

    def halo_copy(side, f):
        return pltpu.make_async_remote_copy(
            src_ref=state_hbm.at[f],
            dst_ref=halo[side][f],
            send_sem=hsend.at[side, f],
            recv_sem=hrecv.at[side, f],
            device_id=sides[side][2],
            device_id_type=MESH,
        )

    def send_halo(fields):
        for f in fields:
            for side in range(2):

                @pl.when(sides[side][1])
                def _():
                    halo_copy(side, f).start()

    send_halo(ORDER[0])
    loads[0].wait()
    loads[1].wait()

    def fill_rows(k, least):
        at = rows_of(k)
        to = pl.ds(pl.multiple_of(k * ROWS + PAD, ROWS), ROWS)
        for layer in range(2):
            w = [state[f, layer, at, :] for f in range(6)]
            q = primitives(w)
            u = q["u"]
            for f in range(6):
                wide[f, layer, to, :] = w[f]
            for i, x in enumerate(u + [q["p"], q["cs"], q["mu"], q["h"], q["nu"]]):
                wide[6 + i, layer, to, :] = x
            speed = (jnp.abs(u[0]) + q["cs"]) + (jnp.abs(u[1]) + q["cs"]) + (jnp.abs(u[2]) + q["cs"])
            least = jnp.minimum(least, volume[layer, at, :] / speed)
        return least

    def fill(k, least):
        for i in range(4):
            least = fill_rows(4 * k + i, least)
        return least

    limit = lax.fori_loop(0, STEPS // 4, fill, jnp.full((ROWS, FACE), jnp.inf, jnp.float32))
    for layer in range(2):
        for i in range(14):
            first_row = wide[i, layer, PAD : PAD + 1, :]
            last_row = wide[i, layer, PAD + FACE - 1 : PAD + FACE, :]
            wide[i, layer, PAD - 2 : PAD - 1, :] = first_row
            wide[i, layer, PAD - 1 : PAD, :] = first_row
            wide[i, layer, PAD + FACE : PAD + FACE + 1, :] = last_row
            wide[i, layer, PAD + FACE + 1 : PAD + FACE + 2, :] = last_row

    send(0, 0, limit)
    for fields in ORDER[1:]:
        send_halo(fields)

    lane = lax.broadcasted_iota(jnp.int32, (ROWS, FACE), 1)
    row = lax.broadcasted_iota(jnp.int32, (ROWS, FACE), 0)
    first, last, top = lane == 0, lane == FACE - 1, row == 0

    def after(x):
        return jnp.where(last, x, pltpu.roll(x, FACE - 1, 1))

    def before(x):
        return jnp.where(first, x, pltpu.roll(x, 1, 1))

    def local_rows(layer, fields, vorticity):
        def load(i, k, offset):
            return wide[i, layer, pl.ds(k * ROWS + PAD + offset, ROWS), :]

        def cell(k, offset):
            v = [load(6 + i, k, offset) for i in range(8)]
            return {"u": v[:3], "p": v[3], "cs": v[4], "mu": v[5], "h": v[6], "nu": v[7]}

        def states(k, offset):
            return [load(f, k, offset) for f in range(6)]

        def body(k, carry):
            w0, q0 = states(k, 0), cell(k, 0)
            w1, q1 = states(k, 1), cell(k, 1)
            pm, p2 = load(9, k, -1), load(9, k, 2)
            s0 = sensor(pm, q0["p"], q1["p"])
            s1 = sensor(q0["p"], q1["p"], p2)
            g = face_flux(2, states(k, -1), w0, w1, states(k, 2), q0, q1, s0, s1, fields)
            turned = [pltpu.roll(x, 1, 0) for x in g]
            total = [x - jnp.where(top, c, y) for x, y, c in zip(g, turned, carry)]
            w1 = [after(x) for x in w0]
            w2 = [after(x) for x in w1]
            wm = [before(x) for x in w0]
            q1 = {n: after(q0[n]) for n in ("p", "cs", "mu", "h", "nu")}
            q1["u"] = [after(x) for x in q0["u"]]
            s0 = sensor(before(q0["p"]), q0["p"], q1["p"])
            g = face_flux(3, wm, w0, w1, w2, q0, q1, s0, after(s0), fields)
            edge = edge_flux(3, w0, w1, q0, s0, fields)
            total = [
                t + (x - jnp.where(first, e, pltpu.roll(x, 1, 1)))
                for t, x, e in zip(total, g, edge)
            ]
            at = rows_of(k)
            for f, x in zip(fields, total):
                part[f, layer, at, :] = x
            if vorticity:
                u1 = [load(6, k, 1), load(8, k, 1)]
                d2u0 = 0.5 * (u1[0] - load(6, k, -1))
                d2u2 = 0.5 * (u1[1] - load(8, k, -1))
                d3u0 = 0.5 * (q1["u"][0] - before(q0["u"][0]))
                d3u1 = 0.5 * (q1["u"][1] - before(q0["u"][1]))
                vort[0, layer, at, :] = d2u2 - d3u1
                vort[1, layer, at, :] = d3u0
                vort[2, layer, at, :] = d2u0
            return tuple(turned)

        def start():
            w0, q0 = states(0, 0), cell(0, 0)
            s0 = sensor(load(9, 0, -1), q0["p"], load(9, 0, 1))
            return tuple(edge_flux(2, w0, states(0, 1), q0, s0, fields))

        return body, start

    def local_flux(fields, vorticity, low, high, group, carry=None):
        layers = [local_rows(layer, fields, vorticity) for layer in range(2)]

        def body(k, carry):
            for i in range(group):
                carry = tuple(layers[l][0](group * k + i, carry[l]) for l in range(2))
            return carry

        if carry is None:
            carry = tuple(start() for _, start in layers)
        return lax.fori_loop(low // group, high // group, body, carry)

    local_flux((0,), False, 0, STEPS, 2)

    def one_if(condition):
        return jnp.where(condition, 1, 0)

    loads[2].wait()
    up = jnp.minimum(blk + 1, chain - 1)
    t, r2, r3 = [flags[i, comp, blk] * one_if(has_below) for i in range(3)]
    lower = (t, t * r3 + (1 - t) * r2, t * r2 + (1 - t) * r3)
    upper = tuple(flags[i, comp, up] * one_if(has_above) for i in range(3))

    turns = []
    for t, flip_rows, flip_lanes in (lower, upper):
        masks = [jnp.broadcast_to(x, (ROWS, FACE)) > 0 for x in (t, flip_rows, flip_lanes)]
        signs = [1.0 - 2.0 * x.astype(jnp.float32) for x in (flip_rows, flip_lanes)]
        turns.append((masks, signs))

    def arrive(fields):
        for side in range(2):
            for f in fields:

                @pl.when(sides[side][0])
                def _():
                    halo_copy(side, f).wait_recv()

                @pl.when(jnp.logical_not(sides[side][0]))
                def _():
                    for layer in range(2):
                        halo[side][f][layer] = state[f, side]

        for side in range(2):
            (turn, reverse_rows, reverse_lanes), signs = turns[side]
            for f in fields:
                for layer in range(2):
                    turned = halo[side][{2: 3, 3: 2}.get(f, f)][layer].T
                    x = []
                    for k in range(STEPS):
                        at = slice(k * ROWS, (k + 1) * ROWS)
                        x.append(jnp.where(turn, turned[at], halo[side][f][layer, at, :]))
                    for k in range(STEPS):
                        y = jnp.take_along_axis(x[STEPS - 1 - k], ROWS - 1 - row, axis=0)
                        y = jnp.where(reverse_rows, y, x[k])
                        z = jnp.take_along_axis(y, FACE - 1 - lane, axis=1)
                        y = jnp.where(reverse_lanes, z, y)
                        if f in (2, 3):
                            y = y * signs[f - 2]
                        ghost[side, f, layer, k * ROWS : (k + 1) * ROWS, :] = y

    arrive(ORDER[0])
    arrive(ORDER[1])
    send(0, 1, receive(0, 0, jnp.minimum))
    arrive(ORDER[2])
    arrive(ORDER[3])

    def own(i, layer, k):
        return wide[i, layer, pl.ds(pl.multiple_of(k * ROWS + PAD, ROWS), ROWS), :]

    def density_rows(k, total):
        at = rows_of(k)
        rho, p, un, cs = [], [], [], []
        for side, layer in ((0, 0), (0, 1), (None, 0), (None, 1), (1, 0), (1, 1)):
            if side is None:
                rho.append(own(0, layer, k))
                un.append(own(6, layer, k))
                p.append(own(9, layer, k))
                cs.append(own(10, layer, k))
            else:
                w = [ghost[side, f, layer, at, :] for f in range(5)]
                q = primitives(w + [w[0]])
                rho.append(w[0])
                un.append(q["u"][0])
                p.append(q["p"])
                cs.append(q["cs"])
        s = [None] + [sensor(p[i - 1], p[i], p[i + 1]) for i in range(1, 5)]
        g = []
        for i in range(1, 4):
            half = 0.5 * ((jnp.abs(un[i]) + cs[i]) + (jnp.abs(un[i + 1]) + cs[i + 1]))
            e2 = 0.25 * jnp.maximum(s[i], s[i + 1])
            b = half * jnp.maximum(0.0, 0.03125 - e2)
            c = half * e2 + 3.0 * b
            g.append(
                0.5 * (rho[i] * un[i] + rho[i + 1] * un[i + 1])
                - c * (rho[i + 1] - rho[i])
                + b * (rho[i + 2] - rho[i - 1])
            )
        for layer in range(2):
            z = (part[0, layer, at, :] + (g[layer + 1] - g[layer])) / volume[layer, at, :]
            change[0, layer, at, :] = z
            total = total + z * z
        return total

    def density(k, total):
        return density_rows(2 * k + 1, density_rows(2 * k, total))

    total = lax.fori_loop(0, STEPS // 2, density, jnp.zeros((ROWS, FACE), jnp.float32))
    send(1, 0, total)
    send(0, 2, receive(0, 1, jnp.minimum))
    arrive(ORDER[4])

    def rest(k, _):
        at = rows_of(k)
        w, q = [], []
        for side, layer in ((0, 0), (0, 1), (None, 0), (None, 1), (1, 0), (1, 1)):
            if side is None:
                w.append([own(f, layer, k) for f in range(6)])
                v = [own(6 + i, layer, k) for i in range(8)]
                q.append({"u": v[:3], "p": v[3], "cs": v[4], "mu": v[5], "h": v[6], "nu": v[7]})
            else:
                w.append([ghost[side, f, layer, at, :] for f in range(6)])
                q.append(primitives(w[-1]))
        s = [None] + [sensor(q[i - 1]["p"], q[i]["p"], q[i + 1]["p"]) for i in range(1, 5)]
        fields = range(1, 6)
        g = [
            face_flux(1, w[i - 1], w[i], w[i + 1], w[i + 2], q[i], q[i + 1], s[i], s[i + 1], fields)
            for i in range(1, 4)
        ]
        for layer in range(2):
            i = layer + 2
            vol = volume[layer, at, :]
            inv = 1.0 / vol
            d1u1 = 0.5 * (q[i + 1]["u"][1] - q[i - 1]["u"][1])
            d1u2 = 0.5 * (q[i + 1]["u"][2] - q[i - 1]["u"][2])
            w1 = vort[0, layer, at, :]
            w2 = vort[1, layer, at, :] - d1u2
            w3 = d1u1 - vort[2, layer, at, :]
            spin = jnp.sqrt(w1 * w1 + w2 * w2 + w3 * w3 + 1e-6)
            ratio = q[i]["nu"] / distance[layer, at, :]
            source = 0.1355 * spin * w[i][5] - 3.239 * w[i][0] * (ratio * ratio)
            for f in fields:
                r = part[f, layer, at, :] + (g[layer + 1][f - 1] - g[layer][f - 1])
                if f == 5:
                    r = r - vol * source
                change[f, layer, at, :] = base[f, layer, at, :] - least * (r * inv)
            change[0, layer, at, :] = base[0, layer, at, :] - least * change[0, layer, at, :]
        return 0

    others = (1, 2, 3, 4, 5)
    held = local_flux(others, True, 0, 2, 1)
    send(1, 1, receive(1, 0, jnp.add))
    local_flux(others, True, 2, STEPS, 1, held)
    send(1, 2, receive(1, 1, jnp.add))
    least = receive(0, 2, jnp.minimum)
    least = jnp.broadcast_to(jnp.min(least, axis=(0, 1), keepdims=True), (ROWS, FACE))
    loads[3].wait()
    loads[4].wait()
    lax.fori_loop(0, STEPS, rest, 0)
    for side in range(2):
        for f in range(6):

            @pl.when(sides[side][1])
            def _():
                halo_copy(side, f).wait_send()

    for kind in range(2):
        for n in range(3):
            seven = slots.at[kind, n, pl.ds(0, 7)]
            pltpu.make_async_copy(seven, seven, rsend.at[kind, n]).wait()
    cells = lax.axis_size("comp") * chain * 2 * FACE * FACE
    norm = jnp.sum(receive(1, 2, jnp.add), axis=(0, 1), keepdims=True)
    total_out[...] = jnp.sqrt(norm / cells)


def entry(*args):
    names = ("flags", "state", "base", "volume", "distance", "wide", "part", "vort")
    names = names + ("ghost", "slots")
    refs = {"inputs": args[:5], "outputs": args[5:7]}
    refs.update(zip(names, args[7:17]))
    refs["halo"] = args[17:29]
    refs["sems"] = args[29:]
    kernel(refs)


def per_device(base_state, section_state, volume, distance, orientation):
    f32 = functools.partial(jax.ShapeDtypeStruct, dtype=jnp.float32)
    scratch = functools.partial(VMEM, dtype=jnp.float32)
    hbm = pl.BlockSpec(memory_space=pl.ANY)
    plane = (2, FACE, FACE)
    dma = pltpu.SemaphoreType.DMA
    flags = jnp.transpose(orientation, (2, 0, 1))
    new, total = pl.pallas_call(
        entry,
        out_shape=(scratch((6,) + plane), f32((1, 1))),
        in_specs=[hbm] * 5,
        out_specs=(pl.BlockSpec(memory_space=VMEM),) * 2,
        scratch_shapes=[
            pltpu.SMEM(flags.shape, jnp.int32),
            scratch((6,) + plane),
            scratch((6,) + plane),
            scratch(plane),
            scratch(plane),
            scratch((14, 2, FACE + 2 * PAD, FACE)),
            scratch((6,) + plane),
            scratch((3,) + plane),
            scratch((2, 6) + plane),
            scratch((2, 3, 8, 8, FACE)),
        ]
        + [scratch(plane)] * 12
        + [dma((5,)), dma((2, 6)), dma((2, 6)), dma((2, 3)), dma((2, 3))],
        compiler_params=pltpu.CompilerParams(collective_id=1, has_side_effects=True),
        cost_estimate=pl.CostEstimate(
            flops=80_000_000, bytes_accessed=4_000_000, transcendentals=800_000
        ),
        name="section",
    )(flags, section_state[0, 0], volume[0, 0], distance[0, 0], base_state[0, 0])
    return new[None, None], total[0, 0]


def solution(mesh):
    wide = P("comp", "blk", None, None, None, None)
    cell = P("comp", "blk", None, None, None)
    return jax.shard_map(
        per_device,
        mesh=mesh,
        in_specs=(wide, wide, cell, cell, P()),
        out_specs=(wide, P()),
        check_vma=False,
    )
```

```python
import functools

import jax
import jax.numpy as jnp
from jax import lax
from jax.experimental import pallas as pl
from jax.experimental.pallas import tpu as pltpu
from jax.sharding import PartitionSpec as P

GAMMA = 1.4
HEAT = 1.4 / (0.4 * 0.72)
CUBE = 7.1 * 7.1 * 7.1
MESH = pl.DeviceIdType.MESH
VMEM = pltpu.VMEM
FACE = 128
PAD = 8


def primitives(w):
    inv = 1.0 / w[0]
    u = [w[1] * inv, w[2] * inv, w[3] * inv]
    kinetic = 0.5 * (w[1] * u[0] + w[2] * u[1] + w[3] * u[2])
    p = 0.4 * (w[4] - kinetic)
    heat = p * inv
    cs = jnp.sqrt(GAMMA * heat)
    chi = w[5] * 20.0
    cubed = chi * chi * chi
    mu = w[5] * cubed / (cubed + CUBE)
    h = 0.5 * (u[0] * u[0] + u[1] * u[1] + u[2] * u[2]) + HEAT * heat
    return {"u": u, "p": p, "cs": cs, "mu": mu, "h": h, "nu": w[5] * inv}


def sensor(before, middle, after):
    twice = 2.0 * middle
    total = after + before
    return jnp.abs(total - twice) / (total + twice)


def face_flux(a, wm, w0, w1, w2, q0, q1, s0, s1, fields=range(6)):
    un0, un1 = q0["u"][a - 1], q1["u"][a - 1]
    half = 0.5 * ((jnp.abs(un0) + q0["cs"]) + (jnp.abs(un1) + q1["cs"]))
    e2 = 0.25 * jnp.maximum(s0, s1)
    e4 = jnp.maximum(0.0, 0.03125 - e2)
    b = half * e4
    c = half * e2 + 3.0 * b
    h0, h1 = 0.5 * un0, 0.5 * un1
    muf = 0.05 + 0.5 * (q0["mu"] + q1["mu"])
    out = []
    for f in fields:
        c0, c1 = w0[f], w1[f]
        if f == 4:
            c0, c1 = c0 + q0["p"], c1 + q1["p"]
        g = c0 * h0 + c1 * h1
        if f == a:
            g = g + 0.5 * (q0["p"] + q1["p"])
        g = g - c * (w1[f] - w0[f]) + b * (w2[f] - wm[f])
        if 1 <= f <= 3:
            g = g - muf * (q1["u"][f - 1] - q0["u"][f - 1])
        elif f == 4:
            g = g - muf * (q1["h"] - q0["h"])
        elif f == 5:
            g = g - (0.075 + 0.75 * (w0[5] + w1[5])) * (q1["nu"] - q0["nu"])
        out.append(g)
    return out


def edge_flux(a, w0, w1, q0, s0, fields=range(6)):
    un = q0["u"][a - 1]
    b = (jnp.abs(un) + q0["cs"]) * jnp.maximum(0.0, 0.03125 - 0.25 * s0)
    out = []
    for f in fields:
        c0 = w0[f] + q0["p"] if f == 4 else w0[f]
        g = c0 * un
        if f == a:
            g = g + q0["p"]
        out.append(g + b * (w1[f] - w0[f]))
    return out


ROWS = 8
STEPS = FACE // ROWS
ORDER = ((2, 3), (0,), (1,), (4,), (5,))


def kernel(refs):
    comp, blk = lax.axis_index("comp"), lax.axis_index("blk")
    chain = lax.axis_size("blk")
    flags_hbm, state_hbm, volume_hbm, distance_hbm, base_hbm = refs["inputs"]
    change, total_out = refs["outputs"]
    flags, base = refs["flags"], refs["base"]
    state, volume, distance = refs["state"], refs["volume"], refs["distance"]
    wide, part, vort = refs["wide"], refs["part"], refs["vort"]
    ghost, slots = refs["ghost"], refs["slots"]
    halo = (refs["halo"][:6], refs["halo"][6:])
    load_sem, hsend, hrecv, rsend, rrecv = refs["sems"]

    low, high = blk % 8, blk // 8
    phases = (
        (low, lambda j: (comp, high * 8 + j)),
        (comp, lambda j: (j, blk)),
        (high, lambda j: (comp, j * 8 + low)),
    )
    has_below, has_above = blk > 0, blk < chain - 1
    below_id = (comp, jnp.maximum(blk - 1, 0))
    above_id = (comp, jnp.minimum(blk + 1, chain - 1))

    loads = [
        pltpu.make_async_copy(source, target, load_sem.at[i])
        for i, (source, target) in enumerate(
            (
                (state_hbm, state),
                (volume_hbm, volume),
                (flags_hbm, flags),
                (distance_hbm, distance),
                (base_hbm, base),
            )
        )
    ]
    for copy in loads:
        copy.start()

    barrier = pltpu.get_barrier_semaphore()
    for has, device in ((has_below, below_id), (has_above, above_id)):

        @pl.when(has)
        def _():
            pl.semaphore_signal(barrier, inc=1, device_id=device, device_id_type=MESH)

    for me, device in phases:
        for step in range(1, 8):
            pl.semaphore_signal(
                barrier, inc=1, device_id=device((me + step) % 8), device_id_type=MESH
            )

    def rows_of(k):
        return pl.ds(pl.multiple_of(k * ROWS, ROWS), ROWS)

    pl.semaphore_wait(
        barrier, 21 + has_below.astype(jnp.int32) + has_above.astype(jnp.int32)
    )

    def exchange(kind, n, step):
        me, device = phases[n]
        return pltpu.make_async_remote_copy(
            src_ref=slots.at[kind, n, me],
            dst_ref=slots.at[kind, n, me],
            send_sem=rsend.at[kind, n],
            recv_sem=rrecv.at[kind, n],
            device_id=device((me + step) % 8),
            device_id_type=MESH,
        )

    def send(kind, n, value):
        slots[kind, n, pl.ds(phases[n][0], 1)] = value[None]
        for step in range(1, 8):
            exchange(kind, n, step).start()

    def receive(kind, n, op):
        seven = slots.at[kind, n, pl.ds(0, 7)]
        pltpu.make_async_copy(seven, seven, rrecv.at[kind, n]).wait()
        held = slots[kind, n, 0]
        for j in range(1, 8):
            held = op(held, slots[kind, n, j])
        return held

    sides = ((has_below, has_above, above_id), (has_above, has_below, below_id))

    def halo_copy(side, f):
        return pltpu.make_async_remote_copy(
            src_ref=state_hbm.at[f],
            dst_ref=halo[side][f],
            send_sem=hsend.at[side, f],
            recv_sem=hrecv.at[side, f],
            device_id=sides[side][2],
            device_id_type=MESH,
        )

    def send_halo(fields):
        for f in fields:
            for side in range(2):

                @pl.when(sides[side][1])
                def _():
                    halo_copy(side, f).start()

    send_halo(ORDER[0])
    loads[0].wait()
    loads[1].wait()

    def fill_rows(k, least):
        at = rows_of(k)
        to = pl.ds(pl.multiple_of(k * ROWS + PAD, ROWS), ROWS)
        for layer in range(2):
            w = [state[f, layer, at, :] for f in range(6)]
            q = primitives(w)
            u = q["u"]
            for f in range(6):
                wide[f, layer, to, :] = w[f]
            for i, x in enumerate(u + [q["p"], q["cs"], q["mu"], q["h"], q["nu"]]):
                wide[6 + i, layer, to, :] = x
            speed = (jnp.abs(u[0]) + q["cs"]) + (jnp.abs(u[1]) + q["cs"]) + (jnp.abs(u[2]) + q["cs"])
            least = jnp.minimum(least, volume[layer, at, :] / speed)
        return least

    def fill(k, least):
        for i in range(4):
            least = fill_rows(4 * k + i, least)
        return least

    limit = lax.fori_loop(0, STEPS // 4, fill, jnp.full((ROWS, FACE), jnp.inf, jnp.float32))
    for layer in range(2):
        for i in range(14):
            first_row = wide[i, layer, PAD : PAD + 1, :]
            last_row = wide[i, layer, PAD + FACE - 1 : PAD + FACE, :]
            wide[i, layer, PAD - 2 : PAD - 1, :] = first_row
            wide[i, layer, PAD - 1 : PAD, :] = first_row
            wide[i, layer, PAD + FACE : PAD + FACE + 1, :] = last_row
            wide[i, layer, PAD + FACE + 1 : PAD + FACE + 2, :] = last_row

    send(0, 0, jnp.min(limit, axis=0, keepdims=True))
    for fields in ORDER[1:]:
        send_halo(fields)

    lane = lax.broadcasted_iota(jnp.int32, (ROWS, FACE), 1)
    row = lax.broadcasted_iota(jnp.int32, (ROWS, FACE), 0)
    first, last, top = lane == 0, lane == FACE - 1, row == 0

    def after(x):
        return jnp.where(last, x, pltpu.roll(x, FACE - 1, 1))

    def before(x):
        return jnp.where(first, x, pltpu.roll(x, 1, 1))

    def local_rows(layer, fields, vorticity):
        def load(i, k, offset):
            return wide[i, layer, pl.ds(k * ROWS + PAD + offset, ROWS), :]

        def cell(k, offset):
            v = [load(6 + i, k, offset) for i in range(8)]
            return {"u": v[:3], "p": v[3], "cs": v[4], "mu": v[5], "h": v[6], "nu": v[7]}

        def states(k, offset):
            return [load(f, k, offset) for f in range(6)]

        def body(k, carry):
            w0, q0 = states(k, 0), cell(k, 0)
            w1, q1 = states(k, 1), cell(k, 1)
            pm, p2 = load(9, k, -1), load(9, k, 2)
            s0 = sensor(pm, q0["p"], q1["p"])
            s1 = sensor(q0["p"], q1["p"], p2)
            g = face_flux(2, states(k, -1), w0, w1, states(k, 2), q0, q1, s0, s1, fields)
            turned = [pltpu.roll(x, 1, 0) for x in g]
            total = [x - jnp.where(top, c, y) for x, y, c in zip(g, turned, carry)]
            w1 = [after(x) for x in w0]
            w2 = [after(x) for x in w1]
            wm = [before(x) for x in w0]
            q1 = {n: after(q0[n]) for n in ("p", "cs", "mu", "h", "nu")}
            q1["u"] = [after(x) for x in q0["u"]]
            s0 = sensor(before(q0["p"]), q0["p"], q1["p"])
            g = face_flux(3, wm, w0, w1, w2, q0, q1, s0, after(s0), fields)
            edge = edge_flux(3, w0, w1, q0, s0, fields)
            total = [
                t + (x - jnp.where(first, e, pltpu.roll(x, 1, 1)))
                for t, x, e in zip(total, g, edge)
            ]
            at = rows_of(k)
            for f, x in zip(fields, total):
                part[f, layer, at, :] = x
            if vorticity:
                u1 = [load(6, k, 1), load(8, k, 1)]
                d2u0 = 0.5 * (u1[0] - load(6, k, -1))
                d2u2 = 0.5 * (u1[1] - load(8, k, -1))
                d3u0 = 0.5 * (q1["u"][0] - before(q0["u"][0]))
                d3u1 = 0.5 * (q1["u"][1] - before(q0["u"][1]))
                vort[0, layer, at, :] = d2u2 - d3u1
                vort[1, layer, at, :] = d3u0
                vort[2, layer, at, :] = d2u0
            return tuple(turned)

        def start():
            w0, q0 = states(0, 0), cell(0, 0)
            s0 = sensor(load(9, 0, -1), q0["p"], load(9, 0, 1))
            return tuple(edge_flux(2, w0, states(0, 1), q0, s0, fields))

        return body, start

    def local_flux(fields, vorticity, low, high, group, carry=None):
        layers = [local_rows(layer, fields, vorticity) for layer in range(2)]

        def body(k, carry):
            for i in range(group):
                carry = tuple(layers[l][0](group * k + i, carry[l]) for l in range(2))
            return carry

        if carry is None:
            carry = tuple(start() for _, start in layers)
        return lax.fori_loop(low // group, high // group, body, carry)

    local_flux((0,), False, 0, STEPS, 2)

    def one_if(condition):
        return jnp.where(condition, 1, 0)

    loads[2].wait()
    up = jnp.minimum(blk + 1, chain - 1)
    t, r2, r3 = [flags[i, comp, blk] * one_if(has_below) for i in range(3)]
    lower = (t, t * r3 + (1 - t) * r2, t * r2 + (1 - t) * r3)
    upper = tuple(flags[i, comp, up] * one_if(has_above) for i in range(3))

    turns = []
    for t, flip_rows, flip_lanes in (lower, upper):
        masks = [jnp.broadcast_to(x, (ROWS, FACE)) > 0 for x in (t, flip_rows, flip_lanes)]
        signs = [1.0 - 2.0 * x.astype(jnp.float32) for x in (flip_rows, flip_lanes)]
        turns.append((masks, signs))

    def arrive(fields):
        for side in range(2):
            for f in fields:

                @pl.when(sides[side][0])
                def _():
                    halo_copy(side, f).wait_recv()

                @pl.when(jnp.logical_not(sides[side][0]))
                def _():
                    for layer in range(2):
                        halo[side][f][layer] = state[f, side]

        for side in range(2):
            (turn, reverse_rows, reverse_lanes), signs = turns[side]
            for f in fields:
                for layer in range(2):
                    turned = halo[side][{2: 3, 3: 2}.get(f, f)][layer].T
                    x = []
                    for k in range(STEPS):
                        at = slice(k * ROWS, (k + 1) * ROWS)
                        x.append(jnp.where(turn, turned[at], halo[side][f][layer, at, :]))
                    for k in range(STEPS):
                        y = jnp.take_along_axis(x[STEPS - 1 - k], ROWS - 1 - row, axis=0)
                        y = jnp.where(reverse_rows, y, x[k])
                        z = jnp.take_along_axis(y, FACE - 1 - lane, axis=1)
                        y = jnp.where(reverse_lanes, z, y)
                        if f in (2, 3):
                            y = y * signs[f - 2]
                        ghost[side, f, layer, k * ROWS : (k + 1) * ROWS, :] = y

    arrive(ORDER[0])
    arrive(ORDER[1])
    send(0, 1, receive(0, 0, jnp.minimum))
    arrive(ORDER[2])
    arrive(ORDER[3])

    def own(i, layer, k):
        return wide[i, layer, pl.ds(pl.multiple_of(k * ROWS + PAD, ROWS), ROWS), :]

    def density_rows(k, total):
        at = rows_of(k)
        rho, p, un, cs = [], [], [], []
        for side, layer in ((0, 0), (0, 1), (None, 0), (None, 1), (1, 0), (1, 1)):
            if side is None:
                rho.append(own(0, layer, k))
                un.append(own(6, layer, k))
                p.append(own(9, layer, k))
                cs.append(own(10, layer, k))
            else:
                w = [ghost[side, f, layer, at, :] for f in range(5)]
                q = primitives(w + [w[0]])
                rho.append(w[0])
                un.append(q["u"][0])
                p.append(q["p"])
                cs.append(q["cs"])
        s = [None] + [sensor(p[i - 1], p[i], p[i + 1]) for i in range(1, 5)]
        g = []
        for i in range(1, 4):
            half = 0.5 * ((jnp.abs(un[i]) + cs[i]) + (jnp.abs(un[i + 1]) + cs[i + 1]))
            e2 = 0.25 * jnp.maximum(s[i], s[i + 1])
            b = half * jnp.maximum(0.0, 0.03125 - e2)
            c = half * e2 + 3.0 * b
            g.append(
                0.5 * (rho[i] * un[i] + rho[i + 1] * un[i + 1])
                - c * (rho[i + 1] - rho[i])
                + b * (rho[i + 2] - rho[i - 1])
            )
        for layer in range(2):
            z = (part[0, layer, at, :] + (g[layer + 1] - g[layer])) / volume[layer, at, :]
            change[0, layer, at, :] = z
            total = total + z * z
        return total

    def density(k, total):
        return density_rows(2 * k + 1, density_rows(2 * k, total))

    total = lax.fori_loop(0, STEPS // 2, density, jnp.zeros((ROWS, FACE), jnp.float32))
    send(1, 0, jnp.sum(total, axis=0, keepdims=True))
    send(0, 2, receive(0, 1, jnp.minimum))
    arrive(ORDER[4])

    def rest(k, _):
        at = rows_of(k)
        w, q = [], []
        for side, layer in ((0, 0), (0, 1), (None, 0), (None, 1), (1, 0), (1, 1)):
            if side is None:
                w.append([own(f, layer, k) for f in range(6)])
                v = [own(6 + i, layer, k) for i in range(8)]
                q.append({"u": v[:3], "p": v[3], "cs": v[4], "mu": v[5], "h": v[6], "nu": v[7]})
            else:
                w.append([ghost[side, f, layer, at, :] for f in range(6)])
                q.append(primitives(w[-1]))
        s = [None] + [sensor(q[i - 1]["p"], q[i]["p"], q[i + 1]["p"]) for i in range(1, 5)]
        fields = range(1, 6)
        g = [
            face_flux(1, w[i - 1], w[i], w[i + 1], w[i + 2], q[i], q[i + 1], s[i], s[i + 1], fields)
            for i in range(1, 4)
        ]
        for layer in range(2):
            i = layer + 2
            vol = volume[layer, at, :]
            inv = 1.0 / vol
            d1u1 = 0.5 * (q[i + 1]["u"][1] - q[i - 1]["u"][1])
            d1u2 = 0.5 * (q[i + 1]["u"][2] - q[i - 1]["u"][2])
            w1 = vort[0, layer, at, :]
            w2 = vort[1, layer, at, :] - d1u2
            w3 = d1u1 - vort[2, layer, at, :]
            spin = jnp.sqrt(w1 * w1 + w2 * w2 + w3 * w3 + 1e-6)
            ratio = q[i]["nu"] / distance[layer, at, :]
            source = 0.1355 * spin * w[i][5] - 3.239 * w[i][0] * (ratio * ratio)
            for f in fields:
                r = part[f, layer, at, :] + (g[layer + 1][f - 1] - g[layer][f - 1])
                if f == 5:
                    r = r - vol * source
                change[f, layer, at, :] = base[f, layer, at, :] - least * (r * inv)
            change[0, layer, at, :] = base[0, layer, at, :] - least * change[0, layer, at, :]
        return 0

    others = (1, 2, 3, 4, 5)
    held = local_flux(others, True, 0, 2, 1)
    send(1, 1, receive(1, 0, jnp.add))
    local_flux(others, True, 2, STEPS, 1, held)
    send(1, 2, receive(1, 1, jnp.add))
    least = receive(0, 2, jnp.minimum)
    least = jnp.broadcast_to(jnp.min(least, axis=(0, 1), keepdims=True), (ROWS, FACE))
    loads[3].wait()
    loads[4].wait()
    lax.fori_loop(0, STEPS, rest, 0)
    for side in range(2):
        for f in range(6):

            @pl.when(sides[side][1])
            def _():
                halo_copy(side, f).wait_send()

    for kind in range(2):
        for n in range(3):
            seven = slots.at[kind, n, pl.ds(0, 7)]
            pltpu.make_async_copy(seven, seven, rsend.at[kind, n]).wait()
    cells = lax.axis_size("comp") * chain * 2 * FACE * FACE
    norm = jnp.sum(receive(1, 2, jnp.add), axis=(0, 1), keepdims=True)
    total_out[...] = jnp.sqrt(norm / cells)


def entry(*args):
    names = ("flags", "state", "base", "volume", "distance", "wide", "part", "vort")
    names = names + ("ghost", "slots")
    refs = {"inputs": args[:5], "outputs": args[5:7]}
    refs.update(zip(names, args[7:17]))
    refs["halo"] = args[17:29]
    refs["sems"] = args[29:]
    kernel(refs)


def per_device(base_state, section_state, volume, distance, orientation):
    f32 = functools.partial(jax.ShapeDtypeStruct, dtype=jnp.float32)
    scratch = functools.partial(VMEM, dtype=jnp.float32)
    hbm = pl.BlockSpec(memory_space=pl.ANY)
    plane = (2, FACE, FACE)
    dma = pltpu.SemaphoreType.DMA
    flags = jnp.transpose(orientation, (2, 0, 1))
    new, total = pl.pallas_call(
        entry,
        out_shape=(scratch((6,) + plane), f32((1, 1))),
        in_specs=[hbm] * 5,
        out_specs=(pl.BlockSpec(memory_space=VMEM),) * 2,
        scratch_shapes=[
            pltpu.SMEM(flags.shape, jnp.int32),
            scratch((6,) + plane),
            scratch((6,) + plane),
            scratch(plane),
            scratch(plane),
            scratch((14, 2, FACE + 2 * PAD, FACE)),
            scratch((6,) + plane),
            scratch((3,) + plane),
            scratch((2, 6) + plane),
            scratch((2, 3, 8, 1, FACE)),
        ]
        + [scratch(plane)] * 12
        + [dma((5,)), dma((2, 6)), dma((2, 6)), dma((2, 3)), dma((2, 3))],
        compiler_params=pltpu.CompilerParams(collective_id=1, has_side_effects=True),
        cost_estimate=pl.CostEstimate(
            flops=80_000_000, bytes_accessed=4_000_000, transcendentals=800_000
        ),
        name="section",
    )(flags, section_state[0, 0], volume[0, 0], distance[0, 0], base_state[0, 0])
    return new[None, None], total[0, 0]


def solution(mesh):
    wide = P("comp", "blk", None, None, None, None)
    cell = P("comp", "blk", None, None, None)
    return jax.shard_map(
        per_device,
        mesh=mesh,
        in_specs=(wide, wide, cell, cell, P()),
        out_specs=(wide, P()),
        check_vma=False,
    )
```

```python
import functools

import jax
import jax.numpy as jnp
from jax import lax
from jax.experimental import pallas as pl
from jax.experimental.pallas import tpu as pltpu
from jax.sharding import PartitionSpec as P

GAMMA = 1.4
HEAT = 1.4 / (0.4 * 0.72)
CUBE = 7.1 * 7.1 * 7.1
MESH = pl.DeviceIdType.MESH
VMEM = pltpu.VMEM
FACE = 128
PAD = 8


def primitives(w):
    inv = 1.0 / w[0]
    u = [w[1] * inv, w[2] * inv, w[3] * inv]
    kinetic = 0.5 * (w[1] * u[0] + w[2] * u[1] + w[3] * u[2])
    p = 0.4 * (w[4] - kinetic)
    heat = p * inv
    cs = jnp.sqrt(GAMMA * heat)
    chi = w[5] * 20.0
    cubed = chi * chi * chi
    mu = w[5] * cubed / (cubed + CUBE)
    h = 0.5 * (u[0] * u[0] + u[1] * u[1] + u[2] * u[2]) + HEAT * heat
    return {"u": u, "p": p, "cs": cs, "mu": mu, "h": h, "nu": w[5] * inv}


def sensor(before, middle, after):
    twice = 2.0 * middle
    total = after + before
    return jnp.abs(total - twice) / (total + twice)


def face_flux(a, wm, w0, w1, w2, q0, q1, s0, s1, fields=range(6)):
    un0, un1 = q0["u"][a - 1], q1["u"][a - 1]
    half = 0.5 * ((jnp.abs(un0) + q0["cs"]) + (jnp.abs(un1) + q1["cs"]))
    e2 = 0.25 * jnp.maximum(s0, s1)
    e4 = jnp.maximum(0.0, 0.03125 - e2)
    b = half * e4
    c = half * e2 + 3.0 * b
    h0, h1 = 0.5 * un0, 0.5 * un1
    muf = 0.05 + 0.5 * (q0["mu"] + q1["mu"])
    out = []
    for f in fields:
        c0, c1 = w0[f], w1[f]
        if f == 4:
            c0, c1 = c0 + q0["p"], c1 + q1["p"]
        g = c0 * h0 + c1 * h1
        if f == a:
            g = g + 0.5 * (q0["p"] + q1["p"])
        g = g - c * (w1[f] - w0[f]) + b * (w2[f] - wm[f])
        if 1 <= f <= 3:
            g = g - muf * (q1["u"][f - 1] - q0["u"][f - 1])
        elif f == 4:
            g = g - muf * (q1["h"] - q0["h"])
        elif f == 5:
            g = g - (0.075 + 0.75 * (w0[5] + w1[5])) * (q1["nu"] - q0["nu"])
        out.append(g)
    return out


def edge_flux(a, w0, w1, q0, s0, fields=range(6)):
    un = q0["u"][a - 1]
    b = (jnp.abs(un) + q0["cs"]) * jnp.maximum(0.0, 0.03125 - 0.25 * s0)
    out = []
    for f in fields:
        c0 = w0[f] + q0["p"] if f == 4 else w0[f]
        g = c0 * un
        if f == a:
            g = g + q0["p"]
        out.append(g + b * (w1[f] - w0[f]))
    return out


ROWS = 8
STEPS = FACE // ROWS
ORDER = ((2, 3), (0,), (1,), (4,), (5,))


def kernel(refs):
    comp, blk = lax.axis_index("comp"), lax.axis_index("blk")
    chain = lax.axis_size("blk")
    flags_hbm, state_hbm, volume_hbm, distance_hbm, base_hbm = refs["inputs"]
    change, total_out = refs["outputs"]
    flags, base = refs["flags"], refs["base"]
    state, volume, distance = refs["state"], refs["volume"], refs["distance"]
    wide, part, vort = refs["wide"], refs["part"], refs["vort"]
    ghost, slots = refs["ghost"], refs["slots"]
    halo = (refs["halo"][:6], refs["halo"][6:])
    load_sem, hsend, hrecv, rsend, rrecv = refs["sems"]

    low, high = blk % 8, blk // 8
    phases = (
        (low, lambda j: (comp, high * 8 + j)),
        (comp, lambda j: (j, blk)),
        (high, lambda j: (comp, j * 8 + low)),
    )
    has_below, has_above = blk > 0, blk < chain - 1
    below_id = (comp, jnp.maximum(blk - 1, 0))
    above_id = (comp, jnp.minimum(blk + 1, chain - 1))

    loads = [
        pltpu.make_async_copy(source, target, load_sem.at[i])
        for i, (source, target) in enumerate(
            (
                (state_hbm, state),
                (volume_hbm, volume),
                (flags_hbm, flags),
                (distance_hbm, distance),
                (base_hbm, base),
            )
        )
    ]
    for copy in loads:
        copy.start()

    barrier = pltpu.get_barrier_semaphore()
    for me, device in phases[::-1]:
        for step in (4, 3, 5, 2, 6, 1, 7):
            pl.semaphore_signal(
                barrier, inc=1, device_id=device((me + step) % 8), device_id_type=MESH
            )
    for has, device in ((has_below, below_id), (has_above, above_id)):

        @pl.when(has)
        def _():
            pl.semaphore_signal(barrier, inc=1, device_id=device, device_id_type=MESH)


    def rows_of(k):
        return pl.ds(pl.multiple_of(k * ROWS, ROWS), ROWS)

    pl.semaphore_wait(
        barrier, 21 + has_below.astype(jnp.int32) + has_above.astype(jnp.int32)
    )

    def exchange(kind, n, step):
        me, device = phases[n]
        return pltpu.make_async_remote_copy(
            src_ref=slots.at[kind, n, me],
            dst_ref=slots.at[kind, n, me],
            send_sem=rsend.at[kind, n],
            recv_sem=rrecv.at[kind, n],
            device_id=device((me + step) % 8),
            device_id_type=MESH,
        )

    def send(kind, n, value):
        slots[kind, n, pl.ds(phases[n][0], 1)] = value[None]
        for step in (4, 3, 5, 2, 6, 1, 7):
            exchange(kind, n, step).start()

    def receive(kind, n, op):
        seven = slots.at[kind, n, pl.ds(0, 7)]
        pltpu.make_async_copy(seven, seven, rrecv.at[kind, n]).wait()
        held = slots[kind, n, 0]
        for j in range(1, 8):
            held = op(held, slots[kind, n, j])
        return held

    sides = ((has_below, has_above, above_id), (has_above, has_below, below_id))

    def halo_copy(side, f):
        return pltpu.make_async_remote_copy(
            src_ref=state_hbm.at[f],
            dst_ref=halo[side][f],
            send_sem=hsend.at[side, f],
            recv_sem=hrecv.at[side, f],
            device_id=sides[side][2],
            device_id_type=MESH,
        )

    def send_halo(fields):
        for f in fields:
            for side in range(2):

                @pl.when(sides[side][1])
                def _():
                    halo_copy(side, f).start()

    send_halo(ORDER[0])
    loads[0].wait()
    loads[1].wait()

    def fill_rows(k, least):
        at = rows_of(k)
        to = pl.ds(pl.multiple_of(k * ROWS + PAD, ROWS), ROWS)
        for layer in range(2):
            w = [state[f, layer, at, :] for f in range(6)]
            q = primitives(w)
            u = q["u"]
            for f in range(6):
                wide[f, layer, to, :] = w[f]
            for i, x in enumerate(u + [q["p"], q["cs"], q["mu"], q["h"], q["nu"]]):
                wide[6 + i, layer, to, :] = x
            speed = (jnp.abs(u[0]) + q["cs"]) + (jnp.abs(u[1]) + q["cs"]) + (jnp.abs(u[2]) + q["cs"])
            least = jnp.minimum(least, volume[layer, at, :] / speed)
        return least

    def fill(k, least):
        for i in range(4):
            least = fill_rows(4 * k + i, least)
        return least

    limit = lax.fori_loop(0, STEPS // 4, fill, jnp.full((ROWS, FACE), jnp.inf, jnp.float32))
    for layer in range(2):
        for i in range(14):
            first_row = wide[i, layer, PAD : PAD + 1, :]
            last_row = wide[i, layer, PAD + FACE - 1 : PAD + FACE, :]
            wide[i, layer, PAD - 2 : PAD - 1, :] = first_row
            wide[i, layer, PAD - 1 : PAD, :] = first_row
            wide[i, layer, PAD + FACE : PAD + FACE + 1, :] = last_row
            wide[i, layer, PAD + FACE + 1 : PAD + FACE + 2, :] = last_row

    send(0, 0, jnp.min(limit, axis=0, keepdims=True))
    for fields in ORDER[1:]:
        send_halo(fields)

    lane = lax.broadcasted_iota(jnp.int32, (ROWS, FACE), 1)
    row = lax.broadcasted_iota(jnp.int32, (ROWS, FACE), 0)
    first, last, top = lane == 0, lane == FACE - 1, row == 0

    def after(x):
        return jnp.where(last, x, pltpu.roll(x, FACE - 1, 1))

    def before(x):
        return jnp.where(first, x, pltpu.roll(x, 1, 1))

    def local_rows(layer, fields, vorticity):
        def load(i, k, offset):
            return wide[i, layer, pl.ds(k * ROWS + PAD + offset, ROWS), :]

        def cell(k, offset):
            v = [load(6 + i, k, offset) for i in range(8)]
            return {"u": v[:3], "p": v[3], "cs": v[4], "mu": v[5], "h": v[6], "nu": v[7]}

        def states(k, offset):
            return [load(f, k, offset) for f in range(6)]

        def body(k, carry):
            w0, q0 = states(k, 0), cell(k, 0)
            w1, q1 = states(k, 1), cell(k, 1)
            pm, p2 = load(9, k, -1), load(9, k, 2)
            s0 = sensor(pm, q0["p"], q1["p"])
            s1 = sensor(q0["p"], q1["p"], p2)
            g = face_flux(2, states(k, -1), w0, w1, states(k, 2), q0, q1, s0, s1, fields)
            turned = [pltpu.roll(x, 1, 0) for x in g]
            total = [x - jnp.where(top, c, y) for x, y, c in zip(g, turned, carry)]
            w1 = [after(x) for x in w0]
            w2 = [after(x) for x in w1]
            wm = [before(x) for x in w0]
            q1 = {n: after(q0[n]) for n in ("p", "cs", "mu", "h", "nu")}
            q1["u"] = [after(x) for x in q0["u"]]
            s0 = sensor(before(q0["p"]), q0["p"], q1["p"])
            g = face_flux(3, wm, w0, w1, w2, q0, q1, s0, after(s0), fields)
            edge = edge_flux(3, w0, w1, q0, s0, fields)
            total = [
                t + (x - jnp.where(first, e, pltpu.roll(x, 1, 1)))
                for t, x, e in zip(total, g, edge)
            ]
            at = rows_of(k)
            for f, x in zip(fields, total):
                part[f, layer, at, :] = x
            if vorticity:
                u1 = [load(6, k, 1), load(8, k, 1)]
                d2u0 = 0.5 * (u1[0] - load(6, k, -1))
                d2u2 = 0.5 * (u1[1] - load(8, k, -1))
                d3u0 = 0.5 * (q1["u"][0] - before(q0["u"][0]))
                d3u1 = 0.5 * (q1["u"][1] - before(q0["u"][1]))
                vort[0, layer, at, :] = d2u2 - d3u1
                vort[1, layer, at, :] = d3u0
                vort[2, layer, at, :] = d2u0
            return tuple(turned)

        def start():
            w0, q0 = states(0, 0), cell(0, 0)
            s0 = sensor(load(9, 0, -1), q0["p"], load(9, 0, 1))
            return tuple(edge_flux(2, w0, states(0, 1), q0, s0, fields))

        return body, start

    def local_flux(fields, vorticity, low, high, group, carry=None):
        layers = [local_rows(layer, fields, vorticity) for layer in range(2)]

        def body(k, carry):
            for i in range(group):
                carry = tuple(layers[l][0](group * k + i, carry[l]) for l in range(2))
            return carry

        if carry is None:
            carry = tuple(start() for _, start in layers)
        return lax.fori_loop(low // group, high // group, body, carry)

    local_flux((0,), False, 0, STEPS, 2)

    def one_if(condition):
        return jnp.where(condition, 1, 0)

    loads[2].wait()
    up = jnp.minimum(blk + 1, chain - 1)
    t, r2, r3 = [flags[i, comp, blk] * one_if(has_below) for i in range(3)]
    lower = (t, t * r3 + (1 - t) * r2, t * r2 + (1 - t) * r3)
    upper = tuple(flags[i, comp, up] * one_if(has_above) for i in range(3))

    turns = []
    for t, flip_rows, flip_lanes in (lower, upper):
        masks = [jnp.broadcast_to(x, (ROWS, FACE)) > 0 for x in (t, flip_rows, flip_lanes)]
        signs = [1.0 - 2.0 * x.astype(jnp.float32) for x in (flip_rows, flip_lanes)]
        turns.append((masks, signs))

    def arrive(fields):
        for side in range(2):
            for f in fields:

                @pl.when(sides[side][0])
                def _():
                    halo_copy(side, f).wait_recv()

                @pl.when(jnp.logical_not(sides[side][0]))
                def _():
                    for layer in range(2):
                        halo[side][f][layer] = state[f, side]

        for side in range(2):
            (turn, reverse_rows, reverse_lanes), signs = turns[side]
            for f in fields:
                for layer in range(2):
                    turned = halo[side][{2: 3, 3: 2}.get(f, f)][layer].T
                    x = []
                    for k in range(STEPS):
                        at = slice(k * ROWS, (k + 1) * ROWS)
                        x.append(jnp.where(turn, turned[at], halo[side][f][layer, at, :]))
                    for k in range(STEPS):
                        y = jnp.take_along_axis(x[STEPS - 1 - k], ROWS - 1 - row, axis=0)
                        y = jnp.where(reverse_rows, y, x[k])
                        z = jnp.take_along_axis(y, FACE - 1 - lane, axis=1)
                        y = jnp.where(reverse_lanes, z, y)
                        if f in (2, 3):
                            y = y * signs[f - 2]
                        ghost[side, f, layer, k * ROWS : (k + 1) * ROWS, :] = y

    arrive(ORDER[0])
    arrive(ORDER[1])
    send(0, 1, receive(0, 0, jnp.minimum))
    arrive(ORDER[2])

    def prepare(k, _):
        for at in (rows_of(2 * k), rows_of(2 * k + 1)):
            for side in range(2):
                for layer in range(2):
                    w = [ghost[side, f, layer, at, :] for f in range(4)]
                    inv = 1.0 / w[0]
                    kinetic = w[1] * (w[1] * inv) + w[2] * (w[2] * inv) + w[3] * (w[3] * inv)
                    ghost[side, 6, layer, at, :] = 0.5 * kinetic
                    ghost[side, 7, layer, at, :] = w[1] * inv
                    ghost[side, 8, layer, at, :] = inv
        return 0

    lax.fori_loop(0, STEPS // 2, prepare, 0)
    arrive(ORDER[3])

    def own(i, layer, k):
        return wide[i, layer, pl.ds(pl.multiple_of(k * ROWS + PAD, ROWS), ROWS), :]

    def density_rows(k, total):
        at = rows_of(k)
        rho, p, un, cs = [], [], [], []
        for side, layer in ((0, 0), (0, 1), (None, 0), (None, 1), (1, 0), (1, 1)):
            if side is None:
                rho.append(own(0, layer, k))
                un.append(own(6, layer, k))
                p.append(own(9, layer, k))
                cs.append(own(10, layer, k))
            else:
                energy, kinetic = ghost[side, 4, layer, at, :], ghost[side, 6, layer, at, :]
                rho.append(ghost[side, 0, layer, at, :])
                un.append(ghost[side, 7, layer, at, :])
                p.append(0.4 * (energy - kinetic))
                cs.append(jnp.sqrt(GAMMA * (p[-1] * ghost[side, 8, layer, at, :])))
        s = [None] + [sensor(p[i - 1], p[i], p[i + 1]) for i in range(1, 5)]
        g = []
        for i in range(1, 4):
            half = 0.5 * ((jnp.abs(un[i]) + cs[i]) + (jnp.abs(un[i + 1]) + cs[i + 1]))
            e2 = 0.25 * jnp.maximum(s[i], s[i + 1])
            b = half * jnp.maximum(0.0, 0.03125 - e2)
            c = half * e2 + 3.0 * b
            g.append(
                0.5 * (rho[i] * un[i] + rho[i + 1] * un[i + 1])
                - c * (rho[i + 1] - rho[i])
                + b * (rho[i + 2] - rho[i - 1])
            )
        for layer in range(2):
            z = (part[0, layer, at, :] + (g[layer + 1] - g[layer])) / volume[layer, at, :]
            change[0, layer, at, :] = z
            total = total + z * z
        return total

    def density(k, total):
        return density_rows(2 * k + 1, density_rows(2 * k, total))

    total = lax.fori_loop(0, STEPS // 2, density, jnp.zeros((ROWS, FACE), jnp.float32))
    send(1, 0, jnp.sum(total, axis=0, keepdims=True))
    send(0, 2, receive(0, 1, jnp.minimum))
    arrive(ORDER[4])

    def rest(k, _):
        at = rows_of(k)
        w, q = [], []
        for side, layer in ((0, 0), (0, 1), (None, 0), (None, 1), (1, 0), (1, 1)):
            if side is None:
                w.append([own(f, layer, k) for f in range(6)])
                v = [own(6 + i, layer, k) for i in range(8)]
                q.append({"u": v[:3], "p": v[3], "cs": v[4], "mu": v[5], "h": v[6], "nu": v[7]})
            else:
                w.append([ghost[side, f, layer, at, :] for f in range(6)])
                q.append(primitives(w[-1]))
        s = [None] + [sensor(q[i - 1]["p"], q[i]["p"], q[i + 1]["p"]) for i in range(1, 5)]
        fields = range(1, 6)
        g = [
            face_flux(1, w[i - 1], w[i], w[i + 1], w[i + 2], q[i], q[i + 1], s[i], s[i + 1], fields)
            for i in range(1, 4)
        ]
        for layer in range(2):
            i = layer + 2
            vol = volume[layer, at, :]
            inv = 1.0 / vol
            d1u1 = 0.5 * (q[i + 1]["u"][1] - q[i - 1]["u"][1])
            d1u2 = 0.5 * (q[i + 1]["u"][2] - q[i - 1]["u"][2])
            w1 = vort[0, layer, at, :]
            w2 = vort[1, layer, at, :] - d1u2
            w3 = d1u1 - vort[2, layer, at, :]
            spin = jnp.sqrt(w1 * w1 + w2 * w2 + w3 * w3 + 1e-6)
            ratio = q[i]["nu"] / distance[layer, at, :]
            source = 0.1355 * spin * w[i][5] - 3.239 * w[i][0] * (ratio * ratio)
            for f in fields:
                r = part[f, layer, at, :] + (g[layer + 1][f - 1] - g[layer][f - 1])
                if f == 5:
                    r = r - vol * source
                change[f, layer, at, :] = base[f, layer, at, :] - least * (r * inv)
            change[0, layer, at, :] = base[0, layer, at, :] - least * change[0, layer, at, :]
        return 0

    others = (1, 2, 3, 4, 5)
    held = local_flux(others, True, 0, 2, 1)
    send(1, 1, receive(1, 0, jnp.add))
    local_flux(others, True, 2, STEPS, 1, held)
    send(1, 2, receive(1, 1, jnp.add))
    least = receive(0, 2, jnp.minimum)
    least = jnp.broadcast_to(jnp.min(least, axis=(0, 1), keepdims=True), (ROWS, FACE))
    loads[3].wait()
    loads[4].wait()
    lax.fori_loop(0, STEPS, rest, 0)
    for side in range(2):
        for f in range(6):

            @pl.when(sides[side][1])
            def _():
                halo_copy(side, f).wait_send()

    for kind in range(2):
        for n in range(3):
            seven = slots.at[kind, n, pl.ds(0, 7)]
            pltpu.make_async_copy(seven, seven, rsend.at[kind, n]).wait()
    cells = lax.axis_size("comp") * chain * 2 * FACE * FACE
    norm = jnp.sum(receive(1, 2, jnp.add), axis=(0, 1), keepdims=True)
    total_out[...] = jnp.sqrt(norm / cells)


def entry(*args):
    names = ("flags", "state", "base", "volume", "distance", "wide", "part", "vort")
    names = names + ("ghost", "slots")
    refs = {"inputs": args[:5], "outputs": args[5:7]}
    refs.update(zip(names, args[7:17]))
    refs["halo"] = args[17:29]
    refs["sems"] = args[29:]
    kernel(refs)


def per_device(base_state, section_state, volume, distance, orientation):
    f32 = functools.partial(jax.ShapeDtypeStruct, dtype=jnp.float32)
    scratch = functools.partial(VMEM, dtype=jnp.float32)
    hbm = pl.BlockSpec(memory_space=pl.ANY)
    plane = (2, FACE, FACE)
    dma = pltpu.SemaphoreType.DMA
    flags = jnp.transpose(orientation, (2, 0, 1))
    new, total = pl.pallas_call(
        entry,
        out_shape=(scratch((6,) + plane), f32((1, 1))),
        in_specs=[hbm] * 5,
        out_specs=(pl.BlockSpec(memory_space=VMEM),) * 2,
        scratch_shapes=[
            pltpu.SMEM(flags.shape, jnp.int32),
            scratch((6,) + plane),
            scratch((6,) + plane),
            scratch(plane),
            scratch(plane),
            scratch((14, 2, FACE + 2 * PAD, FACE)),
            scratch((6,) + plane),
            scratch((3,) + plane),
            scratch((2, 9) + plane),
            scratch((2, 3, 8, 1, FACE)),
        ]
        + [scratch(plane)] * 12
        + [dma((5,)), dma((2, 6)), dma((2, 6)), dma((2, 3)), dma((2, 3))],
        compiler_params=pltpu.CompilerParams(collective_id=1, has_side_effects=True),
        cost_estimate=pl.CostEstimate(
            flops=80_000_000, bytes_accessed=4_000_000, transcendentals=800_000
        ),
        name="section",
    )(flags, section_state[0, 0], volume[0, 0], distance[0, 0], base_state[0, 0])
    return new[None, None], total[0, 0]


def solution(mesh):
    wide = P("comp", "blk", None, None, None, None)
    cell = P("comp", "blk", None, None, None)
    return jax.shard_map(
        per_device,
        mesh=mesh,
        in_specs=(wide, wide, cell, cell, P()),
        out_specs=(wide, P()),
        check_vma=False,
    )
```
